256 devices in a mesh: shards: 16 (over x, y), tensor: 4 (over z_hi, core), replica: 4 (over z_lo).
Axes of the slice: x: 4, y: 4, z: 8 (z_hi: 2, z_lo: 4; z = z_hi * 4 + z_lo), core: 2. Of those that a mesh axis runs over, the one named last changes fastest.
Arguments:
- activations: bfloat16 [262144, 1024], P(('shards', 'tensor', 'replica')), may hold values from -24 to 24
- grads_out: bfloat16 [262144, 1024], P(('shards', 'tensor', 'replica')), may hold values from -24 to 24
- grad_parts: float32 [64, 1024, 1024], P(('shards', 'replica'), None, 'tensor'), may hold values from -80 to 80
- old_factors: float32 [16, 128, 128], replicated, may hold values from -16 to 16, as said below
- block_owner: int32 [16], replicated, may hold values from 0 to 15, as said below
- weights: float32 [1024, 1024], P(('shards', 'replica'), 'tensor'), may hold values from -0.1875 to 0.1875
- momentum: float32 [1024, 1024], P(('shards', 'replica'), 'tensor'), may hold values from -4 to 4
Outputs:
- weights_next: float32 [1024, 1024], P(None, 'tensor')
- momentum_next: float32 [1024, 1024], P(('shards', 'replica'), 'tensor')
- next_factor_blocks: float32 [32, 128, 128], P('shards')
The draws below stay inside these ranges and needn't reach their ends.
Inputs may be any that keep to these rules, and one draw needn't show every extreme that they name: `block_owner`: each shard index owns at most 2 of the 16 blocks, and some index owns exactly 2. `old_factors`: each block is symmetric and positive definite.
All inputs are finite; a program needn't handle non-finite values. Where the reference program divides by a largest or mean magnitude, that divisor is 1e-20 or more.
Results may differ from the reference program's by a relative error of at most 0.0003.
Values sent between devices are 32-bit elements; how exact they have to be, the bound alone decides.
No kernel may reach another device: no remote copies, remote signals or barrier semaphores. Data moves between devices by JAX's collectives and lax.ppermute only.
A program may use at most 64 MiB of HBM per device.

```python
import math
import jax
import jax.numpy as jnp
from jax import lax

D = 1024
D_OUT = 1024
BLOCK_ORDER_SIZE = 128
NS_STEPS = 4
TOK_DEV = 1024
TOKENS = 262144
DATA = 64
NBLK = 16
BLOCKS_PER_SHARD = 2
OWNER_SLOT_TOTAL = 32


def draw_grad_parts(key, part):
    first_key = jax.random.fold_in(key, 11)
    row_frac = jnp.arange(D, dtype=jnp.float32) / D
    row_rise = jnp.power(3.0, row_frac)
    normal_part = jnp.clip(jax.random.normal(first_key, (DATA, D, D_OUT), jnp.float32), -6.0, 6.0)
    return normal_part * row_rise[None, :, None]


def draw_old_factors(key, part):
    first_key = jax.random.fold_in(key, 21)
    second_key = jax.random.fold_in(key, 22)
    diagonal = jnp.exp(jax.random.uniform(first_key, (NBLK, BLOCK_ORDER_SIZE), jnp.float32, 0.0, math.log(4.0)))
    uniform_part = jax.random.uniform(second_key, (NBLK, BLOCK_ORDER_SIZE, BLOCK_ORDER_SIZE), jnp.float32, -1.0, 1.0)
    symmetric = 0.5 * (uniform_part + jnp.transpose(uniform_part, (0, 2, 1)))
    root_diag = jnp.sqrt(diagonal)
    identity = jnp.eye(BLOCK_ORDER_SIZE, dtype=jnp.float32)
    off_part = symmetric * (0.9 / BLOCK_ORDER_SIZE) * root_diag[:, :, None] * root_diag[:, None, :]
    return off_part * (1.0 - identity) + diagonal[:, :, None] * identity


def draw_block_owner(key, part):
    block_owner_list = OWNER_SLOT_TOTAL // BLOCKS_PER_SHARD
    first_key = jax.random.fold_in(key, 31)
    second_key = jax.random.fold_in(key, 32)
    third_key = jax.random.fold_in(key, 33)
    busiest = jax.random.randint(first_key, (), 0, block_owner_list)
    block_order = jax.random.permutation(second_key, NBLK)
    others = jax.random.permutation(third_key, (block_owner_list - 1) * BLOCKS_PER_SHARD)[:NBLK - BLOCKS_PER_SHARD] // BLOCKS_PER_SHARD
    others = others + (others >= busiest).astype(jnp.int32)
    assigned = jnp.concatenate([jnp.full((BLOCKS_PER_SHARD,), busiest, jnp.int32), others.astype(jnp.int32)])
    return jnp.zeros((NBLK,), jnp.int32).at[block_order].set(assigned)


def with_spikes(values, stream_key, source, target, blocks, factor):
    def block_of(axis_at):
        return (jnp.arange(values.shape[axis_at]) // (values.shape[axis_at] // blocks)).reshape((-1,) + (1,) * (values.ndim - 1 - axis_at))

    one_side = jax.random.permutation(stream_key, blocks)[block_of(target)]
    other_side = (block_of(target) + blocks // 2) % blocks
    return jnp.where((block_of(source) == one_side) | (block_of(source) == other_side), factor * values, values)


def block_levels(key, shape, split, low, top_value):
    gain = 1.0
    for axis_at, shards_of in split:
        heights = jax.random.uniform(jax.random.fold_in(jax.random.fold_in(key, 6), axis_at), (shards_of,), jnp.float32, low / len(split), top_value / len(split))
        gain = gain * jnp.repeat(jnp.exp(heights), shape[axis_at] // shards_of).reshape((-1,) + (1,) * (len(shape) - 1 - axis_at))
    return gain


def bell_draw(stream_key, dims, scale, most, shards=(), held_as=jnp.bfloat16):
    gain = block_levels(stream_key, dims, shards, -0.22, 0.18) if shards else 1.0
    array = jax.random.normal(stream_key, dims, jnp.float32) * scale * gain
    return jnp.minimum(jnp.maximum(array, -most), most).astype(held_as)


def bell_draw_with(key, extent, spread, reach, cuts, heavy, held_as=jnp.bfloat16):
    array = spread * jax.random.normal(key, extent, jnp.float32)
    if cuts:
        array = array * block_levels(key, extent, cuts, -0.22, 0.18)
    return jnp.clip(with_spikes(array, jax.random.fold_in(key, 3), *heavy), -reach, reach).astype(held_as)


def setup_inputs(seed: int = 0) -> dict:
    key_list = jax.random.split(jax.random.key(seed), 8)
    return {
        "activations": bell_draw_with(key_list[0], (TOKENS, D), 1.0, 24.0, ((0, 256),), (0, 1, 256, 6.0)),
        "grads_out": bell_draw_with(key_list[1], (TOKENS, D_OUT), 1.0, 24.0, ((0, 256),), (0, 1, 256, 6.0)),
        "grad_parts": draw_grad_parts(jax.random.fold_in(key_list[7], 71), 0),
        "old_factors": draw_old_factors(jax.random.fold_in(key_list[7], 71), 0),
        "block_owner": draw_block_owner(jax.random.fold_in(key_list[7], 71), 0),
        "weights": bell_draw(key_list[5], (D, D_OUT), D ** -0.5, 0.1875, ((0, 64), (1, 4)), jnp.float32),
        "momentum": bell_draw(key_list[6], (D, D_OUT), 0.3, 4.0, ((0, 64), (1, 4)), jnp.float32),
    }


exact_mode = lax.Precision.HIGHEST
decay_rate = 0.75
damping = 0.1
damp_shift = 0.001
clip_norm = 256.0
momentum_rate = 0.9
step_rate = 0.05

def block_stats(samples):
    block_count = samples.shape[1] // BLOCK_ORDER_SIZE
    pieces = samples.reshape(-1, TOK_DEV, block_count, BLOCK_ORDER_SIZE)

    def accumulate(summed, shard_piece):
        widened = shard_piece.astype(jnp.float32)
        return (summed + jnp.einsum('tnb,tnc->nbc', widened, widened, precision=exact_mode), None)
    summed, _ = lax.scan(accumulate, jnp.zeros((block_count, BLOCK_ORDER_SIZE, BLOCK_ORDER_SIZE), jnp.float32), pieces)
    return summed

def newton_inverse(mixed_factor_blocks):
    block_size = mixed_factor_blocks.shape[-1]
    identity = jnp.eye(block_size, dtype=jnp.float32)
    traces = jnp.trace(mixed_factor_blocks, axis1=1, axis2=2)
    damped = mixed_factor_blocks + (damping * traces / block_size + damp_shift)[:, None, None] * identity
    bounds = lax.optimization_barrier(jnp.max(lax.optimization_barrier(jnp.sum(jnp.abs(damped), axis=2)), axis=1))
    approx = identity[None, :, :] / bounds[:, None, None]
    for iteration in range(NS_STEPS):
        left_part = jnp.einsum('nab,nbc->nac', approx, damped, precision=exact_mode)
        approx = 2.0 * approx - jnp.einsum('nab,nbc->nac', left_part, approx, precision=exact_mode)
    return approx

def reference(activations, grads_out, grad_parts, old_factors, block_owner, weights, momentum):
    sample_count = activations.shape[0]
    statistics = jnp.concatenate([block_stats(activations), block_stats(grads_out)], axis=0) / sample_count
    mixed_factor_blocks = decay_rate * old_factors + (1.0 - decay_rate) * statistics
    inverses = newton_inverse(mixed_factor_blocks)
    left_count = D // BLOCK_ORDER_SIZE
    gradient = lax.optimization_barrier(jnp.sum(grad_parts, axis=0))
    left_part = jnp.einsum('nab,nbc->nac', inverses[:left_count], gradient.reshape(left_count, BLOCK_ORDER_SIZE, D_OUT), precision=exact_mode).reshape(D, D_OUT)
    precond = jnp.einsum('rnb,nbc->rnc', left_part.reshape(D, D_OUT // BLOCK_ORDER_SIZE, BLOCK_ORDER_SIZE), inverses[left_count:], precision=exact_mode).reshape(D, D_OUT)
    alignment_sum = jnp.sum(precond * gradient)
    clip_scale = jnp.minimum(1.0, clip_norm / jnp.sqrt(alignment_sum))
    momentum_next = momentum_rate * momentum + clip_scale * precond
    weights_next = weights - step_rate * momentum_next
    positions = jnp.arange(NBLK, dtype=jnp.int32)
    earlier = (block_owner[:, None] == block_owner[None, :]) & (positions[None, :] < positions[:, None])
    owner_slot_list = (block_owner * BLOCKS_PER_SHARD + lax.optimization_barrier(jnp.sum(earlier.astype(jnp.int32), axis=1))).astype(jnp.int32)
    next_factor_blocks = jnp.zeros((OWNER_SLOT_TOTAL, BLOCK_ORDER_SIZE, BLOCK_ORDER_SIZE), jnp.float32).at[owner_slot_list].set(mixed_factor_blocks)
    return (weights_next, momentum_next, next_factor_blocks)
```

```python
import jax
import jax.numpy as jnp
from jax import lax
from jax.sharding import PartitionSpec as P

NS_STEPS = 4


exact_mode = lax.Precision.HIGHEST
decay_rate = 0.75
damping = 0.1
damp_shift = 0.001
clip_norm = 256.0
momentum_rate = 0.9
step_rate = 0.05


def sample_stats(samples, block_size):
    sample_rows, width = samples.shape
    blocks = samples.reshape(sample_rows, width // block_size, block_size)
    return jnp.einsum("tnb,tnc->nbc", blocks, blocks, preferred_element_type=jnp.float32)


def newton_inverse(mixed_factor_blocks):
    block_size = mixed_factor_blocks.shape[-1]
    identity = jnp.eye(block_size, dtype=jnp.float32)
    traces = jnp.trace(mixed_factor_blocks, axis1=1, axis2=2)
    damped = (
        mixed_factor_blocks + (damping * traces / block_size + damp_shift)[:, None, None] * identity
    )
    bounds = jnp.max(jnp.sum(jnp.abs(damped), axis=2), axis=1)
    approx = identity[None, :, :] / bounds[:, None, None]
    for iteration in range(NS_STEPS):
        left_part = jnp.einsum("nab,nbc->nac", approx, damped, precision=exact_mode)
        approx = 2.0 * approx - jnp.einsum("nab,nbc->nac", left_part, approx, precision=exact_mode)
    return approx


def swap(value, axis, flip):
    size = lax.axis_size(axis)
    return lax.ppermute(value, axis, [(i, i ^ flip) for i in range(size)])


def exchange_sum(value, axis):
    parts = [swap(value, axis, flip) for flip in range(1, lax.axis_size(axis))]
    for part in parts:
        value = value + part
    return value


def body(activations, grads_out, grad_parts, old_factors, block_owner, weights, momentum):
    shard_count = lax.axis_size("shards")
    block_count = old_factors.shape[0]
    block_size = old_factors.shape[1]
    capacity = (block_count + shard_count - 1) // shard_count + 1
    sample_count = (
        activations.shape[0] * shard_count * lax.axis_size("tensor") * lax.axis_size("replica")
    )
    partial_grad = grad_parts[0]
    row_count, col_count = partial_grad.shape
    left_count = row_count // block_size
    right_count = col_count // block_size

    base = weights - (step_rate * momentum_rate) * momentum
    base = lax.all_gather(base, "replica", axis=0, tiled=True)
    base = lax.all_gather(base, "shards", axis=0, tiled=True)

    stats = jnp.concatenate(
        [sample_stats(activations, block_size), sample_stats(grads_out, block_size)], axis=0
    )
    piece_rows = row_count // shard_count
    grad_pieces = [
        partial_grad[:, n * block_size : (n + 1) * block_size].reshape(
            shard_count, piece_rows, block_size
        )
        for n in range(right_count)
    ]
    outgoing = jnp.concatenate([stats] + grad_pieces, axis=1)
    incoming = lax.all_to_all(outgoing, "shards", 0, 0)
    summed = exchange_sum(jnp.sum(incoming, axis=0), "replica")
    own_stats = summed[:block_size]
    own_stats = own_stats + swap(own_stats, "tensor", 1)
    own_stats = own_stats + swap(own_stats, "tensor", 2)
    own = jnp.concatenate([own_stats, summed[block_size:]], axis=0)
    own, base = lax.optimization_barrier((own, base))
    gathered = lax.all_to_all(
        jnp.broadcast_to(own[None], (shard_count,) + own.shape), "shards", 0, 0
    )
    blended = decay_rate * old_factors + (1.0 - decay_rate) * (
        gathered[:, :block_size] / sample_count
    )
    grad_columns = [
        gathered[
            :, block_size + n * piece_rows : block_size + (n + 1) * piece_rows
        ].reshape(left_count, block_size, block_size)
        for n in range(right_count)
    ]

    positions = jnp.arange(block_count, dtype=jnp.int32)
    earlier = (block_owner[:, None] == block_owner[None, :]) & (
        positions[None, :] < positions[:, None]
    )
    slots = block_owner * capacity + jnp.sum(earlier.astype(jnp.int32), axis=1)
    owned = []
    for place in range(capacity):
        match = slots == lax.axis_index("shards") * capacity + place
        which = jnp.sum(jnp.where(match, positions, 0))
        block = lax.dynamic_index_in_dim(blended, which, 0, keepdims=False)
        owned.append(jnp.where(jnp.any(match), block, 0.0))
    owned_blocks = jnp.stack(owned)

    right_first = left_count + lax.axis_index("tensor") * right_count
    needed = jnp.concatenate(
        [
            blended[:left_count],
            lax.dynamic_slice_in_dim(blended, right_first, right_count, 0),
        ],
        axis=0,
    )
    inverses = newton_inverse(needed)
    precond_columns = []
    for n in range(right_count):
        left_part = jnp.einsum(
            "nab,nbc->nac", inverses[:left_count], grad_columns[n], precision=exact_mode
        )
        precond_columns.append(
            jnp.einsum("nab,bc->nac", left_part, inverses[left_count + n], precision=exact_mode)
        )
    local_sum = sum(jnp.sum(p * g) for p, g in zip(precond_columns, grad_columns))
    precond = jnp.concatenate(
        [p.reshape(row_count, block_size) for p in precond_columns], axis=1
    )
    alignment_sum = lax.psum(local_sum, "tensor")
    clip_scale = jnp.minimum(1.0, clip_norm / jnp.sqrt(alignment_sum))
    own_rows = weights.shape[0]
    first_row = lax.axis_index(("shards", "replica")) * own_rows
    own_precond = lax.dynamic_slice_in_dim(precond, first_row, own_rows, 0)
    momentum_next = momentum_rate * momentum + clip_scale * own_precond
    weights_next = base - (step_rate * clip_scale) * precond
    return (weights_next, momentum_next, owned_blocks)


def solution(mesh):
    placed = (
        P(("shards", "tensor", "replica"), None),
        P(("shards", "tensor", "replica"), None),
        P(("shards", "replica"), None, "tensor"),
        P(),
        P(),
        P(("shards", "replica"), "tensor"),
        P(("shards", "replica"), "tensor"),
    )
    return jax.shard_map(
        body,
        mesh=mesh,
        in_specs=placed,
        out_specs=(P(None, "tensor"), P(("shards", "replica"), "tensor"), P("shards", None, None)),
        check_vma=False,
    )
```

```python
import jax
import jax.numpy as jnp
from jax import lax
from jax.experimental import pallas as pl
from jax.experimental.pallas import tpu as pltpu
from jax.sharding import PartitionSpec as P

NS_STEPS = 4


exact_mode = lax.Precision.HIGHEST
decay_rate = 0.75
damping = 0.1
damp_shift = 0.001
clip_norm = 256.0
momentum_rate = 0.9
step_rate = 0.05


def sample_stats(samples, block_size):
    sample_rows, width = samples.shape
    blocks = samples.reshape(sample_rows, width // block_size, block_size)
    return jnp.einsum("tnb,tnc->nbc", blocks, blocks, preferred_element_type=jnp.float32)


def pack_kernel(left_ref, right_ref, grad_ref, packed_ref):
    left_count, size, _ = left_ref.shape
    half = size // 2
    chunks = packed_ref.shape[0]
    piece_rows = grad_ref.shape[0] // chunks
    row = lax.broadcasted_iota(jnp.int32, (half, size), 0)
    col = lax.broadcasted_iota(jnp.int32, (half, size), 1)
    for n in range(chunks):
        stats_ref, at = (left_ref, n) if n < left_count else (right_ref, n - left_count)
        top = stats_ref[at, :half, :]
        bottom = stats_ref[at, half:, :]
        packed_ref[n, :half, :] = jnp.where(col >= row, top, pltpu.roll(bottom, half, 1))
        diagonal = jnp.sum(jnp.where(col == row + half, bottom, 0.0), axis=0, keepdims=True)
        packed_ref[n, half : half + 8, :] = jnp.broadcast_to(diagonal, (8, size))
        for c in range(grad_ref.shape[1] // size):
            first = half + 8 + c * piece_rows
            packed_ref[n, first : first + piece_rows, :] = grad_ref[
                n * piece_rows : (n + 1) * piece_rows, c * size : (c + 1) * size
            ]


def pack(left_stats, right_stats, grad):
    left_count, size, _ = left_stats.shape
    chunks = left_count + right_stats.shape[0]
    rows = size // 2 + 8 + grad.size // (chunks * size)
    return pl.pallas_call(
        pack_kernel,
        out_shape=jax.ShapeDtypeStruct((chunks, rows, size), jnp.float32),
        name="pack",
    )(left_stats, right_stats, grad)


def dot(a, b):
    return jnp.dot(a, b, precision=exact_mode, preferred_element_type=jnp.float32)


def damp(mixed, on_diagonal):
    size = mixed.shape[0]
    trace = jnp.sum(jnp.where(on_diagonal, mixed, 0.0), keepdims=True)
    damped = mixed + jnp.where(on_diagonal, damping * trace / size + damp_shift, 0.0)
    bound = jnp.max(jnp.sum(jnp.abs(damped), axis=1, keepdims=True), keepdims=True)
    return jnp.where(on_diagonal, 1.0, 0.0) - damped / bound, bound


def update_kernel(
    sample_count,
    place_ref,
    packed_ref,
    old_ref,
    precond_ref,
    owned_ref,
    align_ref,
    blended_ref,
):
    blocks, size, _ = old_ref.shape
    half = size // 2
    right_count = precond_ref.shape[1] // size
    left_count = precond_ref.shape[0] // size
    piece_rows = precond_ref.shape[0] // blocks
    row = lax.broadcasted_iota(jnp.int32, (half, size), 0)
    col = lax.broadcasted_iota(jnp.int32, (half, size), 1)
    for n in range(blocks):
        part = packed_ref[n, :half, :]
        diagonal = packed_ref[n, half : half + 1, :]
        turned = jnp.concatenate([part, jnp.zeros_like(part)], axis=0).T
        top = jnp.where(col >= row, part, turned[:half])
        corner = jnp.where(
            col < row + half, pltpu.roll(part, half, 1), pltpu.roll(turned[:half], half, 1)
        )
        corner = jnp.where(col == row + half, diagonal, corner)
        bottom = jnp.where(col < half, turned[half:], corner)
        for first, stats in ((0, top), (half, bottom)):
            blended_ref[n, first : first + half, :] = decay_rate * old_ref[
                n, first : first + half, :
            ] + (1.0 - decay_rate) * (stats / sample_count)

    for place in range(owned_ref.shape[0]):
        block = place_ref[1 + place]
        used = block >= 0
        value = blended_ref[jnp.maximum(block, 0)]
        owned_ref[place] = jnp.where(used, value, jnp.zeros_like(value))

    on_diagonal = lax.broadcasted_iota(jnp.int32, (size, size), 0) == lax.broadcasted_iota(
        jnp.int32, (size, size), 1
    )
    needed = [blended_ref[n] for n in range(left_count)]
    needed += [blended_ref[place_ref[0] + n] for n in range(right_count)]
    powers, bounds, inverses = [], [], []
    for mixed in needed:
        power, bound = damp(mixed, on_diagonal)
        powers.append(power)
        bounds.append(bound)
        inverses.append(jnp.where(on_diagonal, 1.0, 0.0) + power)
    for step in range(NS_STEPS - 1):
        powers = [dot(power, power) for power in powers]
        inverses = [x + dot(x, power) for x, power in zip(inverses, powers)]
    inverses = [x / bound for x, bound in zip(inverses, bounds)]

    total = jnp.zeros((size, size), jnp.float32)
    for a in range(left_count):
        for c in range(right_count):
            first = half + 8 + c * piece_rows
            pieces = size // piece_rows
            grad = jnp.concatenate(
                [
                    packed_ref[pieces * a + k, first : first + piece_rows, :]
                    for k in range(pieces)
                ],
                axis=0,
            )
            value = dot(dot(inverses[a], grad), inverses[left_count + c])
            precond_ref[a * size : (a + 1) * size, c * size : (c + 1) * size] = value
            total = total + value * grad
    align_ref[...] = jnp.broadcast_to(jnp.sum(total, keepdims=True), align_ref.shape)


def update(places, packed, old_factors, capacity, rows, cols, sample_count):
    size = old_factors.shape[1]
    return pl.pallas_call(
        lambda *refs: update_kernel(sample_count, *refs),
        in_specs=[
            pl.BlockSpec(memory_space=pltpu.SMEM),
            pl.BlockSpec(memory_space=pltpu.VMEM),
            pl.BlockSpec(memory_space=pltpu.VMEM),
        ],
        out_shape=(
            jax.ShapeDtypeStruct((rows, cols), jnp.float32),
            jax.ShapeDtypeStruct((capacity, size, size), jnp.float32),
            jax.ShapeDtypeStruct((8, 128), jnp.float32),
        ),
        scratch_shapes=[pltpu.VMEM(old_factors.shape, jnp.float32)],
        compiler_params=pltpu.CompilerParams(vmem_limit_bytes=40 * 1024 * 1024),
        name="update",
    )(places, packed, old_factors)


def swap(value, axis, flip):
    size = lax.axis_size(axis)
    return lax.ppermute(value, axis, [(i, i ^ flip) for i in range(size)])


def exchange(value, axis):
    return [value] + [swap(value, axis, flip) for flip in range(1, lax.axis_size(axis))]


def spread(value, axis):
    copies = jnp.broadcast_to(value[None], (lax.axis_size(axis),) + value.shape)
    return lax.all_to_all(copies, axis, 0, 0)


def body(activations, grads_out, grad_parts, old_factors, block_owner, weights, momentum):
    shard_count = lax.axis_size("shards")
    replica_count = lax.axis_size("replica")
    block_count = old_factors.shape[0]
    block_size = old_factors.shape[1]
    capacity = (block_count + shard_count - 1) // shard_count + 1
    sample_count = activations.shape[0] * shard_count * lax.axis_size("tensor") * replica_count
    partial_grad = grad_parts[0]
    row_count, col_count = partial_grad.shape
    left_count = row_count // block_size
    right_count = col_count // block_size
    piece_rows = row_count // shard_count

    outgoing = pack(
        sample_stats(activations, block_size), sample_stats(grads_out, block_size), partial_grad
    )
    incoming = lax.all_to_all(outgoing, "shards", 0, 0)

    base = weights - (step_rate * momentum_rate) * momentum
    base_parts = exchange(base, "replica")
    replica = lax.axis_index("replica")
    base_rows = []
    for place in range(replica_count):
        rows = base_parts[0]
        for flip in range(1, replica_count):
            rows = jnp.where(replica ^ flip == place, base_parts[flip], rows)
        base_rows.append(rows)
    base = lax.all_gather(jnp.concatenate(base_rows, axis=0), "shards", axis=0, tiled=True)

    own = sum(exchange(jnp.sum(incoming, axis=0), "replica"))
    fold_rows = block_size // 2 + 8
    own_stats = own[:fold_rows]
    own_stats = own_stats + swap(own_stats, "tensor", 1)
    own_stats = own_stats + swap(own_stats, "tensor", 2)
    packed = spread(jnp.concatenate([own_stats, own[fold_rows:]], axis=0), "shards")

    positions = jnp.arange(block_count, dtype=jnp.int32)
    earlier = (block_owner[:, None] == block_owner[None, :]) & (
        positions[None, :] < positions[:, None]
    )
    slots = block_owner * capacity + jnp.sum(earlier.astype(jnp.int32), axis=1)
    own_slots = lax.axis_index("shards") * capacity + jnp.arange(capacity, dtype=jnp.int32)
    holds = jnp.max(jnp.where(slots[None, :] == own_slots[:, None], positions[None, :], -1), axis=1)
    right_first = left_count + lax.axis_index("tensor") * right_count
    places = jnp.concatenate([right_first.reshape(1).astype(jnp.int32), holds])

    precond, owned_blocks, align = update(
        places, packed, old_factors, capacity, row_count, col_count, sample_count
    )
    align, base = lax.optimization_barrier((align, base))
    align = align[:1]
    align = align + swap(align, "tensor", 1)
    align = align + swap(align, "tensor", 2)
    clip_scale = jnp.minimum(1.0, clip_norm / jnp.sqrt(align[0, 0]))
    own_rows = weights.shape[0]
    first_row = lax.axis_index(("shards", "replica")) * own_rows
    own_precond = lax.dynamic_slice_in_dim(precond, first_row, own_rows, 0)
    momentum_next = momentum_rate * momentum + clip_scale * own_precond
    weights_next = base - (step_rate * clip_scale) * precond
    return (weights_next, momentum_next, owned_blocks)


def solution(mesh):
    placed = (
        P(("shards", "tensor", "replica"), None),
        P(("shards", "tensor", "replica"), None),
        P(("shards", "replica"), None, "tensor"),
        P(),
        P(),
        P(("shards", "replica"), "tensor"),
        P(("shards", "replica"), "tensor"),
    )
    return jax.shard_map(
        body,
        mesh=mesh,
        in_specs=placed,
        out_specs=(P(None, "tensor"), P(("shards", "replica"), "tensor"), P("shards", None, None)),
        check_vma=False,
    )
```

```python
import jax
import jax.numpy as jnp
from jax import lax
from jax.experimental import pallas as pl
from jax.experimental.pallas import tpu as pltpu
from jax.sharding import PartitionSpec as P

NS_STEPS = 4


exact_mode = lax.Precision.HIGHEST
decay_rate = 0.75
damping = 0.1
damp_shift = 0.001
clip_norm = 256.0
momentum_rate = 0.9
step_rate = 0.05


def sample_stats(samples, block_size):
    sample_rows, width = samples.shape
    blocks = samples.reshape(sample_rows, width // block_size, block_size)
    return jnp.einsum("tnb,tnc->nbc", blocks, blocks, preferred_element_type=jnp.float32)


def fold_kernel(place_ref, left_ref, right_ref, *folded_refs):
    left_count, size, _ = left_ref.shape
    half = size // 2
    side = len(folded_refs)
    row = lax.broadcasted_iota(jnp.int32, (half, size), 0)
    col = lax.broadcasted_iota(jnp.int32, (half, size), 1)
    for k in range(side):
        for j in range(side):
            n = (place_ref[0] ^ k) * side + (place_ref[1] ^ j)
            at = n % left_count
            stats = jnp.where(n < left_count, left_ref[at], right_ref[at])
            top, bottom = stats[:half], stats[half:]
            folded_refs[k][j, :half, :] = jnp.where(col >= row, top, pltpu.roll(bottom, half, 1))
            diagonal = jnp.sum(jnp.where(col == row + half, bottom, 0.0), axis=0, keepdims=True)
            folded_refs[k][j, half:, :] = jnp.broadcast_to(diagonal, (8, size))


def fold(places, left_stats, right_stats, side):
    size = left_stats.shape[1]
    return pl.pallas_call(
        fold_kernel,
        in_specs=[
            pl.BlockSpec(memory_space=pltpu.SMEM),
            pl.BlockSpec(memory_space=pltpu.VMEM),
            pl.BlockSpec(memory_space=pltpu.VMEM),
        ],
        out_shape=[jax.ShapeDtypeStruct((side, size // 2 + 8, size), jnp.float32)] * side,
        name="fold",
    )(places, left_stats, right_stats)


def dot(a, b):
    return jnp.dot(a, b, precision=exact_mode, preferred_element_type=jnp.float32)


def damp(mixed, on_diagonal):
    size = mixed.shape[0]
    trace = jnp.sum(jnp.where(on_diagonal, mixed, 0.0), keepdims=True)
    damped = mixed + jnp.where(on_diagonal, damping * trace / size + damp_shift, 0.0)
    bound = jnp.max(jnp.sum(jnp.abs(damped), axis=1, keepdims=True), keepdims=True)
    return jnp.where(on_diagonal, 1.0, 0.0) - damped / bound, bound


def update_kernel(side, sample_count, place_ref, *refs):
    folded_refs = refs[:side]
    grad_ref, old_ref, precond_ref, owned_ref, align_ref, blended_ref = refs[side:]
    size = old_ref.shape[1]
    half = size // 2
    right_count = precond_ref.shape[1] // size
    left_count = precond_ref.shape[0] // size
    row = lax.broadcasted_iota(jnp.int32, (half, size), 0)
    col = lax.broadcasted_iota(jnp.int32, (half, size), 1)
    for k in range(side):
        for j in range(side):
            n = (place_ref[0] ^ k) * side + (place_ref[1] ^ j)
            part = folded_refs[k][j, :half, :]
            diagonal = folded_refs[k][j, half : half + 1, :]
            turned = jnp.concatenate([part, jnp.zeros_like(part)], axis=0).T
            top = jnp.where(col >= row, part, turned[:half])
            corner = jnp.where(
                col < row + half, pltpu.roll(part, half, 1), pltpu.roll(turned[:half], half, 1)
            )
            corner = jnp.where(col == row + half, diagonal, corner)
            bottom = jnp.where(col < half, turned[half:], corner)
            for first, stats in ((0, top), (half, bottom)):
                blended_ref[n, first : first + half, :] = decay_rate * old_ref[
                    n, first : first + half, :
                ] + (1.0 - decay_rate) * (stats / sample_count)

    for place in range(owned_ref.shape[0]):
        block = place_ref[3 + place]
        used = block >= 0
        value = blended_ref[jnp.maximum(block, 0)]
        owned_ref[place] = jnp.where(used, value, jnp.zeros_like(value))

    on_diagonal = lax.broadcasted_iota(jnp.int32, (size, size), 0) == lax.broadcasted_iota(
        jnp.int32, (size, size), 1
    )
    needed = [blended_ref[n] for n in range(left_count)]
    needed += [blended_ref[place_ref[2] + n] for n in range(right_count)]
    powers, bounds, inverses = [], [], []
    for mixed in needed:
        power, bound = damp(mixed, on_diagonal)
        powers.append(power)
        bounds.append(bound)
        inverses.append(jnp.where(on_diagonal, 1.0, 0.0) + power)
    for step in range(NS_STEPS - 1):
        powers = [dot(power, power) for power in powers]
        inverses = [x + dot(x, power) for x, power in zip(inverses, powers)]
    inverses = [x / bound for x, bound in zip(inverses, bounds)]

    total = jnp.zeros((size, size), jnp.float32)
    for a in range(left_count):
        for c in range(right_count):
            grad = grad_ref[a * size : (a + 1) * size, c * size : (c + 1) * size]
            value = dot(dot(inverses[a], grad), inverses[left_count + c])
            precond_ref[a * size : (a + 1) * size, c * size : (c + 1) * size] = value
            total = total + value * grad
    align_ref[...] = jnp.broadcast_to(jnp.sum(total, keepdims=True), align_ref.shape)


def update(places, folded, gradient, old_factors, capacity, sample_count):
    size = old_factors.shape[1]
    side = len(folded)
    return pl.pallas_call(
        lambda *refs: update_kernel(side, sample_count, *refs),
        in_specs=[pl.BlockSpec(memory_space=pltpu.SMEM)]
        + [pl.BlockSpec(memory_space=pltpu.VMEM)] * (side + 2),
        out_shape=(
            jax.ShapeDtypeStruct(gradient.shape, jnp.float32),
            jax.ShapeDtypeStruct((capacity, size, size), jnp.float32),
            jax.ShapeDtypeStruct((8, 128), jnp.float32),
        ),
        scratch_shapes=[pltpu.VMEM(old_factors.shape, jnp.float32)],
        compiler_params=pltpu.CompilerParams(vmem_limit_bytes=40 * 1024 * 1024),
        name="update",
    )(places, *folded, gradient, old_factors)


def swap(value, axis, flip):
    size = lax.axis_size(axis)
    return lax.ppermute(value, axis, [(i, i ^ flip) for i in range(size)])


def exchange(value, axis):
    return [value] + [swap(value, axis, flip) for flip in range(1, lax.axis_size(axis))]


def spread(value, axis):
    copies = jnp.broadcast_to(value[None], (lax.axis_size(axis),) + value.shape)
    return lax.all_to_all(copies, axis, 0, 0)


def body(activations, grads_out, grad_parts, old_factors, block_owner, weights, momentum):
    shard_count = lax.axis_size("shards")
    replica_count = lax.axis_size("replica")
    block_count = old_factors.shape[0]
    block_size = old_factors.shape[1]
    capacity = (block_count + shard_count - 1) // shard_count + 1
    sample_count = activations.shape[0] * shard_count * lax.axis_size("tensor") * replica_count
    partial_grad = grad_parts[0]
    row_count, col_count = partial_grad.shape
    left_count = row_count // block_size
    right_count = col_count // block_size
    piece_rows = row_count // shard_count

    side = 4
    shard = lax.axis_index("shards")

    grad_in = lax.all_to_all(partial_grad.reshape(shard_count, piece_rows, col_count), "shards", 0, 0)

    coords = jnp.stack([shard // side, shard % side]).astype(jnp.int32)
    along_x = fold(
        coords,
        sample_stats(activations, block_size),
        sample_stats(grads_out, block_size),
        side,
    )
    parts = [along_x[0]] + [swap(along_x[k], "shards", k * side) for k in range(1, side)]
    along_y = [sum(part[j] for part in parts) for j in range(side)]
    own_stats = along_y[0] + sum(swap(along_y[j], "shards", j) for j in range(1, side))

    base = weights - (step_rate * momentum_rate) * momentum
    base_parts = exchange(base, "replica")
    replica = lax.axis_index("replica")
    base_rows = []
    for place in range(replica_count):
        rows = base_parts[0]
        for flip in range(1, replica_count):
            rows = jnp.where(replica ^ flip == place, base_parts[flip], rows)
        base_rows.append(rows)
    base = lax.all_gather(jnp.concatenate(base_rows, axis=0), "shards", axis=0, tiled=True)

    own_grad = sum(exchange(jnp.sum(grad_in, axis=0), "replica"))
    gradient = spread(own_grad, "shards").reshape(row_count, col_count)

    own_stats = own_stats + swap(own_stats, "tensor", 1)
    own_stats = own_stats + swap(own_stats, "replica", 1)
    own_stats = own_stats + swap(own_stats, "replica", 2)
    own_stats = own_stats + swap(own_stats, "tensor", 2)
    row_of_y = jnp.stack([own_stats] + [swap(own_stats, "shards", j) for j in range(1, side)])
    folded = [row_of_y] + [swap(row_of_y, "shards", k * side) for k in range(1, side)]
    gradient, base = lax.optimization_barrier((gradient, base))

    positions = jnp.arange(block_count, dtype=jnp.int32)
    earlier = (block_owner[:, None] == block_owner[None, :]) & (
        positions[None, :] < positions[:, None]
    )
    slots = block_owner * capacity + jnp.sum(earlier.astype(jnp.int32), axis=1)
    own_slots = lax.axis_index("shards") * capacity + jnp.arange(capacity, dtype=jnp.int32)
    holds = jnp.max(jnp.where(slots[None, :] == own_slots[:, None], positions[None, :], -1), axis=1)
    right_first = left_count + lax.axis_index("tensor") * right_count
    places = jnp.concatenate([coords, right_first.reshape(1).astype(jnp.int32), holds])

    precond, owned_blocks, align = update(
        places, folded, gradient, old_factors, capacity, sample_count
    )
    align = align[:1]
    align = align + swap(align, "tensor", 1)
    align = align + swap(align, "tensor", 2)
    clip_scale = jnp.minimum(1.0, clip_norm / jnp.sqrt(align[0, 0]))
    own_rows = weights.shape[0]
    first_row = lax.axis_index(("shards", "replica")) * own_rows
    own_precond = lax.dynamic_slice_in_dim(precond, first_row, own_rows, 0)
    momentum_next = momentum_rate * momentum + clip_scale * own_precond
    weights_next = base - (step_rate * clip_scale) * precond
    return (weights_next, momentum_next, owned_blocks)


def solution(mesh):
    placed = (
        P(("shards", "tensor", "replica"), None),
        P(("shards", "tensor", "replica"), None),
        P(("shards", "replica"), None, "tensor"),
        P(),
        P(),
        P(("shards", "replica"), "tensor"),
        P(("shards", "replica"), "tensor"),
    )
    return jax.shard_map(
        body,
        mesh=mesh,
        in_specs=placed,
        out_specs=(P(None, "tensor"), P(("shards", "replica"), "tensor"), P("shards", None, None)),
        check_vma=False,
    )
```

```python
import jax
import jax.numpy as jnp
from jax import lax
from jax.experimental import pallas as pl
from jax.experimental.pallas import tpu as pltpu
from jax.sharding import PartitionSpec as P

NS_STEPS = 4


exact_mode = lax.Precision.HIGHEST
decay_rate = 0.75
damping = 0.1
damp_shift = 0.001
clip_norm = 256.0
momentum_rate = 0.9
step_rate = 0.05


def sample_stats(samples, block_size):
    sample_rows, width = samples.shape
    blocks = samples.reshape(sample_rows, width // block_size, block_size)
    return jnp.einsum("tnb,tnc->nbc", blocks, blocks, preferred_element_type=jnp.float32)


def fold_kernel(left_ref, right_ref, old_ref, folded_ref, old_folded_ref):
    left_count, size, _ = left_ref.shape
    half = size // 2
    row = lax.broadcasted_iota(jnp.int32, (half, size), 0)
    col = lax.broadcasted_iota(jnp.int32, (half, size), 1)

    def fold_block(from_ref, at, to_ref, to):
        top = from_ref[at, :half, :]
        bottom = from_ref[at, half:, :]
        to_ref[to, :half, :] = jnp.where(col >= row, top, pltpu.roll(bottom, half, 1))
        diagonal = jnp.sum(jnp.where(col == row + half, bottom, 0.0), axis=0, keepdims=True)
        to_ref[to, half:, :] = jnp.broadcast_to(diagonal, (to_ref.shape[1] - half, size))

    def step(n, carry):
        fold_block(left_ref, n, folded_ref, n)
        fold_block(right_ref, n, folded_ref, n + left_count)
        return carry

    lax.fori_loop(0, left_count, step, 0)
    fold_block(old_ref, 0, old_folded_ref, 0)


def fold(left_stats, right_stats, old_block):
    count, size, _ = left_stats.shape
    rows = size // 2 + 8
    return pl.pallas_call(
        fold_kernel,
        out_shape=(
            jax.ShapeDtypeStruct((2 * count, rows, size), jnp.float32),
            jax.ShapeDtypeStruct((1, rows, size), jnp.float32),
        ),
        name="fold",
    )(left_stats, right_stats, old_block)


def dot(a, b):
    return jnp.dot(a, b, precision=exact_mode, preferred_element_type=jnp.float32)


def unfold(part, diagonal):
    half, size = part.shape
    row = lax.broadcasted_iota(jnp.int32, (half, size), 0)
    col = lax.broadcasted_iota(jnp.int32, (half, size), 1)
    turned = jnp.concatenate([part, jnp.zeros_like(part)], axis=0).T
    top = jnp.where(col >= row, part, turned[:half])
    corner = jnp.where(
        col < row + half, pltpu.roll(part, half, 1), pltpu.roll(turned[:half], half, 1)
    )
    corner = jnp.where(col == row + half, diagonal, corner)
    bottom = jnp.where(col < half, turned[half:], corner)
    return jnp.concatenate([top, bottom], axis=0)


def inverse_kernel(group, place_ref, folded_ref, inverse_ref, owned_ref):
    size = inverse_ref.shape[1]
    half = size // 2
    left_count = inverse_ref.shape[0] - place_ref[1]
    on_diagonal = lax.broadcasted_iota(jnp.int32, (size, size), 0) == lax.broadcasted_iota(
        jnp.int32, (size, size), 1
    )
    unit = jnp.where(on_diagonal, 1.0, 0.0)

    def load(block):
        return unfold(folded_ref[block, :half, :], folded_ref[block, half : half + 1, :])

    def invert(step, carry):
        powers, bounds, inverses = [], [], []
        for k in range(group):
            at = step * group + k
            mixed = load(jnp.where(at < left_count, at, place_ref[0] + at - left_count))
            trace = jnp.sum(jnp.where(on_diagonal, mixed, 0.0), keepdims=True)
            damped = mixed + jnp.where(on_diagonal, damping * trace / size + damp_shift, 0.0)
            bound = jnp.max(jnp.sum(jnp.abs(damped), axis=1, keepdims=True), keepdims=True)
            power = unit - damped / bound
            powers.append(power)
            bounds.append(bound)
            inverses.append(unit + power)
        for iteration in range(NS_STEPS - 1):
            powers = [dot(power, power) for power in powers]
            inverses = [x + dot(x, power) for x, power in zip(inverses, powers)]
        for k in range(group):
            inverse_ref[step * group + k] = inverses[k] / bounds[k]
        return carry

    lax.fori_loop(0, inverse_ref.shape[0] // group, invert, 0)

    def place_block(place, carry):
        block = place_ref[2 + place]
        value = load(jnp.maximum(block, 0))
        owned_ref[place] = jnp.where(block >= 0, value, jnp.zeros_like(value))
        return carry

    lax.fori_loop(0, owned_ref.shape[0], place_block, 0)


def invert_needed(places, folded, needed, capacity):
    size = folded.shape[2]
    group = 5
    return pl.pallas_call(
        lambda *refs: inverse_kernel(group, *refs),
        in_specs=[
            pl.BlockSpec(memory_space=pltpu.SMEM),
            pl.BlockSpec(memory_space=pltpu.VMEM),
        ],
        out_shape=(
            jax.ShapeDtypeStruct((needed, size, size), jnp.float32),
            jax.ShapeDtypeStruct((capacity, size, size), jnp.float32),
        ),
        name="inverse",
    )(places, folded)


def precondition_kernel(inverse_ref, grad_ref, precond_ref, align_ref):
    size = inverse_ref.shape[1]
    left_count = grad_ref.shape[0] // size
    right_count = grad_ref.shape[1] // size

    def step(a, total):
        first = pl.multiple_of(a * size, size)
        grad = grad_ref[pl.ds(first, size), :]
        left_part = dot(inverse_ref[a], grad)
        for c in range(right_count):
            cols = slice(c * size, (c + 1) * size)
            value = dot(left_part[:, cols], inverse_ref[left_count + c])
            precond_ref[pl.ds(first, size), cols] = value
            total = total + value * grad[:, cols]
        return total

    total = lax.fori_loop(0, left_count, step, jnp.zeros((size, size), jnp.float32), unroll=2)
    align_ref[...] = jnp.broadcast_to(jnp.sum(total, keepdims=True), align_ref.shape)


def precondition(inverses, gradient):
    return pl.pallas_call(
        precondition_kernel,
        out_shape=(
            jax.ShapeDtypeStruct(gradient.shape, jnp.float32),
            jax.ShapeDtypeStruct((8, 128), jnp.float32),
        ),
        name="precondition",
    )(inverses, gradient)


def swap(value, axis, flip):
    size = lax.axis_size(axis)
    return lax.ppermute(value, axis, [(i, i ^ flip) for i in range(size)])


def exchange(value, axis):
    return [value] + [swap(value, axis, flip) for flip in range(1, lax.axis_size(axis))]


def spread(value, axis):
    copies = jnp.broadcast_to(value[None], (lax.axis_size(axis),) + value.shape)
    return lax.all_to_all(copies, axis, 0, 0)


def body(activations, grads_out, grad_parts, old_factors, block_owner, weights, momentum):
    shard_count = lax.axis_size("shards")
    replica_count = lax.axis_size("replica")
    block_count = old_factors.shape[0]
    block_size = old_factors.shape[1]
    capacity = (block_count + shard_count - 1) // shard_count + 1
    sample_count = activations.shape[0] * shard_count * lax.axis_size("tensor") * replica_count
    partial_grad = grad_parts[0]
    row_count, col_count = partial_grad.shape
    left_count = row_count // block_size
    right_count = col_count // block_size
    piece_rows = row_count // shard_count
    own_rows = weights.shape[0]
    shard = lax.axis_index("shards")
    replica = lax.axis_index("replica")

    grad_in = lax.all_to_all(partial_grad.reshape(shard_count, piece_rows, col_count), "shards", 0, 0)

    old_block = lax.dynamic_slice_in_dim(old_factors, shard, 1, 0)
    folded, old_folded = fold(
        sample_stats(activations, block_size), sample_stats(grads_out, block_size), old_block
    )
    folded, grad_in = lax.optimization_barrier((folded, grad_in))
    stats_in = lax.all_to_all(folded, "shards", 0, 0)

    base = weights - (step_rate * momentum_rate) * momentum
    base_rows = lax.dynamic_update_slice_in_dim(
        jnp.zeros((piece_rows, col_count), jnp.float32), base, replica * own_rows, 0
    )
    own = sum(
        exchange(jnp.concatenate([jnp.sum(grad_in, axis=0), base_rows], axis=0), "replica")
    )
    own_grad = own[:piece_rows]
    base = lax.all_gather(own[piece_rows:], "shards", axis=0, tiled=True)

    own_stats = jnp.sum(stats_in, axis=0)
    own_stats, own_grad = lax.optimization_barrier((own_stats, own_grad))
    gradient = spread(own_grad, "shards").reshape(row_count, col_count)
    own_stats = own_stats + swap(own_stats, "tensor", 1)
    own_stats = sum(exchange(own_stats, "replica"))
    own_stats = own_stats + swap(own_stats, "tensor", 2)
    blended = decay_rate * old_folded[0] + ((1.0 - decay_rate) / sample_count) * own_stats
    blended, gradient = lax.optimization_barrier((blended, gradient))
    folded = spread(blended, "shards")

    positions = jnp.arange(block_count, dtype=jnp.int32)
    earlier = (block_owner[:, None] == block_owner[None, :]) & (
        positions[None, :] < positions[:, None]
    )
    slots = block_owner * capacity + jnp.sum(earlier.astype(jnp.int32), axis=1)
    own_slots = shard * capacity + jnp.arange(capacity, dtype=jnp.int32)
    holds = jnp.max(jnp.where(slots[None, :] == own_slots[:, None], positions[None, :], -1), axis=1)
    right_first = left_count + lax.axis_index("tensor") * right_count
    places = jnp.concatenate(
        [jnp.stack([right_first, jnp.asarray(right_count)]).astype(jnp.int32), holds]
    )
    inverses, owned_blocks = invert_needed(places, folded, left_count + right_count, capacity)
    precond, align = precondition(inverses, gradient)
    align, base = lax.optimization_barrier((align, base))
    align = align[:1]
    align = align + swap(align, "tensor", 1)
    align = align + swap(align, "tensor", 2)
    clip_scale = jnp.minimum(1.0, clip_norm / jnp.sqrt(align[0, 0]))
    first_row = (shard * replica_count + replica) * own_rows
    own_precond = lax.dynamic_slice_in_dim(precond, first_row, own_rows, 0)
    momentum_next = momentum_rate * momentum + clip_scale * own_precond
    weights_next = base - (step_rate * clip_scale) * precond
    return (weights_next, momentum_next, owned_blocks)


def solution(mesh):
    placed = (
        P(("shards", "tensor", "replica"), None),
        P(("shards", "tensor", "replica"), None),
        P(("shards", "replica"), None, "tensor"),
        P(),
        P(),
        P(("shards", "replica"), "tensor"),
        P(("shards", "replica"), "tensor"),
    )
    return jax.shard_map(
        body,
        mesh=mesh,
        in_specs=placed,
        out_specs=(P(None, "tensor"), P(("shards", "replica"), "tensor"), P("shards", None, None)),
        check_vma=False,
    )
```

```python
import jax
import jax.numpy as jnp
from jax import lax
from jax.experimental import pallas as pl
from jax.experimental.pallas import tpu as pltpu
from jax.sharding import PartitionSpec as P

NS_STEPS = 4


exact_mode = lax.Precision.HIGHEST
decay_rate = 0.75
damping = 0.1
damp_shift = 0.001
clip_norm = 256.0
momentum_rate = 0.9
step_rate = 0.05


def sample_stats(samples, block_size):
    sample_rows, width = samples.shape
    blocks = samples.reshape(sample_rows, width // block_size, block_size)
    return jnp.einsum("tnb,tnc->nbc", blocks, blocks, preferred_element_type=jnp.float32)


def fold_block(block, rows):
    size = block.shape[1]
    half = size // 2
    row = lax.broadcasted_iota(jnp.int32, (half, size), 0)
    col = lax.broadcasted_iota(jnp.int32, (half, size), 1)
    top, bottom = block[:half], block[half:]
    triangle = jnp.where(col >= row, top, pltpu.roll(bottom, half, 1))
    diagonal = jnp.sum(jnp.where(col == row + half, bottom, 0.0), axis=0, keepdims=True)
    return triangle, jnp.broadcast_to(diagonal, (rows - half, size))


def fold_kernel(place_ref, left_ref, right_ref, *folded_refs):
    left_count, size, _ = left_ref.shape
    side = len(folded_refs)
    rows = folded_refs[0].shape[1]
    for k in range(side):
        for j in range(side):
            n = (place_ref[0] ^ k) * side + (place_ref[1] ^ j)
            at = n % left_count
            triangle, diagonal = fold_block(
                jnp.where(n < left_count, left_ref[at], right_ref[at]), rows
            )
            folded_refs[k][j, : size // 2, :] = triangle
            folded_refs[k][j, size // 2 :, :] = diagonal


def fold(places, left_stats, right_stats, side):
    size = left_stats.shape[1]
    return pl.pallas_call(
        fold_kernel,
        in_specs=[
            pl.BlockSpec(memory_space=pltpu.SMEM),
            pl.BlockSpec(memory_space=pltpu.VMEM),
            pl.BlockSpec(memory_space=pltpu.VMEM),
        ],
        out_shape=[jax.ShapeDtypeStruct((side, size // 2 + 8, size), jnp.float32)] * side,
        name="fold",
    )(places, left_stats, right_stats)


def fold_one_kernel(block_ref, folded_ref):
    half = block_ref.shape[1] // 2
    triangle, diagonal = fold_block(block_ref[0], folded_ref.shape[0])
    folded_ref[:half, :] = triangle
    folded_ref[half:, :] = diagonal


def fold_one(block):
    size = block.shape[2]
    return pl.pallas_call(
        fold_one_kernel,
        out_shape=jax.ShapeDtypeStruct((size // 2 + 8, size), jnp.float32),
        name="fold_one",
    )(block)


def dot(a, b):
    return jnp.dot(a, b, precision=exact_mode, preferred_element_type=jnp.float32)


def unfold(part, diagonal):
    half, size = part.shape
    row = lax.broadcasted_iota(jnp.int32, (half, size), 0)
    col = lax.broadcasted_iota(jnp.int32, (half, size), 1)
    turned = jnp.concatenate([part, jnp.zeros_like(part)], axis=0).T
    top = jnp.where(col >= row, part, turned[:half])
    corner = jnp.where(
        col < row + half, pltpu.roll(part, half, 1), pltpu.roll(turned[:half], half, 1)
    )
    corner = jnp.where(col == row + half, diagonal, corner)
    bottom = jnp.where(col < half, turned[half:], corner)
    return jnp.concatenate([top, bottom], axis=0)


def update_kernel(side, place_ref, *refs):
    folded_refs = refs[:side]
    grad_ref, precond_ref, owned_ref, align_ref, blended_ref = refs[side:]
    size = blended_ref.shape[2]
    half = blended_ref.shape[1] - 8
    right_count = grad_ref.shape[1] // size
    left_count = grad_ref.shape[0] // size
    for k in range(side):
        for j in range(side):
            n = (place_ref[0] ^ k) * side + (place_ref[1] ^ j)
            blended_ref[n] = folded_refs[k][j]

    def load(block):
        return unfold(blended_ref[block, :half, :], blended_ref[block, half : half + 1, :])

    on_diagonal = lax.broadcasted_iota(jnp.int32, (size, size), 0) == lax.broadcasted_iota(
        jnp.int32, (size, size), 1
    )
    unit = jnp.where(on_diagonal, 1.0, 0.0)
    powers, bounds, inverses = [], [], []
    for block in list(range(left_count)) + [place_ref[2] + n for n in range(right_count)]:
        mixed = load(block)
        trace = jnp.sum(jnp.where(on_diagonal, mixed, 0.0), keepdims=True)
        damped = mixed + jnp.where(on_diagonal, damping * trace / size + damp_shift, 0.0)
        bound = jnp.max(jnp.sum(jnp.abs(damped), axis=1, keepdims=True), keepdims=True)
        power = unit - damped / bound
        powers.append(power)
        bounds.append(bound)
        inverses.append(unit + power)
    for step in range(NS_STEPS - 1):
        powers = [dot(power, power) for power in powers]
        inverses = [x + dot(x, power) for x, power in zip(inverses, powers)]
    inverses = [x / bound for x, bound in zip(inverses, bounds)]

    total = jnp.zeros((size, size), jnp.float32)
    for a in range(left_count):
        rows = slice(a * size, (a + 1) * size)
        left_part = dot(inverses[a], grad_ref[rows, :])
        for c in range(right_count):
            cols = slice(c * size, (c + 1) * size)
            value = dot(left_part[:, cols], inverses[left_count + c])
            precond_ref[rows, cols] = value
            total = total + value * grad_ref[rows, cols]
    align_ref[...] = jnp.broadcast_to(jnp.sum(total, keepdims=True), align_ref.shape)

    for place in range(owned_ref.shape[0]):
        block = place_ref[3 + place]
        value = load(jnp.maximum(block, 0))
        owned_ref[place] = jnp.where(block >= 0, value, jnp.zeros_like(value))


def update(places, folded, gradient, capacity):
    side, rows, size = folded[0].shape
    return pl.pallas_call(
        lambda *refs: update_kernel(side, *refs),
        in_specs=[pl.BlockSpec(memory_space=pltpu.SMEM)]
        + [pl.BlockSpec(memory_space=pltpu.VMEM)] * (side + 1),
        out_shape=(
            jax.ShapeDtypeStruct(gradient.shape, jnp.float32),
            jax.ShapeDtypeStruct((capacity, size, size), jnp.float32),
            jax.ShapeDtypeStruct((1, size), jnp.float32),
        ),
        scratch_shapes=[pltpu.VMEM((side * side, rows, size), jnp.float32)],
        compiler_params=pltpu.CompilerParams(vmem_limit_bytes=40 * 1024 * 1024),
        name="update",
    )(places, *folded, gradient)


def swap(value, axis, flip):
    size = lax.axis_size(axis)
    return lax.ppermute(value, axis, [(i, i ^ flip) for i in range(size)])


def exchange(value, axis):
    return [value] + [swap(value, axis, flip) for flip in range(1, lax.axis_size(axis))]


def spread(value, axis):
    copies = jnp.broadcast_to(value[None], (lax.axis_size(axis),) + value.shape)
    return lax.all_to_all(copies, axis, 0, 0)


def body(activations, grads_out, grad_parts, old_factors, block_owner, weights, momentum):
    shard_count = lax.axis_size("shards")
    replica_count = lax.axis_size("replica")
    block_count = old_factors.shape[0]
    block_size = old_factors.shape[1]
    capacity = (block_count + shard_count - 1) // shard_count + 1
    sample_count = activations.shape[0] * shard_count * lax.axis_size("tensor") * replica_count
    partial_grad = grad_parts[0]
    row_count, col_count = partial_grad.shape
    left_count = row_count // block_size
    right_count = col_count // block_size
    piece_rows = row_count // shard_count
    own_rows = weights.shape[0]
    shard = lax.axis_index("shards")
    replica = lax.axis_index("replica")

    grad_in = lax.all_to_all(partial_grad.reshape(shard_count, piece_rows, col_count), "shards", 0, 0)

    side = 4
    coords = jnp.stack([shard // side, shard % side]).astype(jnp.int32)
    along_x = fold(
        coords,
        sample_stats(activations, block_size),
        sample_stats(grads_out, block_size),
        side,
    )
    parts = [along_x[0]] + [swap(along_x[k], "shards", k * side) for k in range(1, side)]
    along_y = [sum(part[j] for part in parts) for j in range(side)]
    along_y, grad_in = lax.optimization_barrier((along_y, grad_in))
    own_stats = along_y[0] + sum(swap(along_y[j], "shards", j) for j in range(1, side))

    base = weights - (step_rate * momentum_rate) * momentum
    base_rows = lax.dynamic_update_slice_in_dim(
        jnp.zeros((piece_rows, col_count), jnp.float32), base, replica * own_rows, 0
    )
    own_parts = exchange(jnp.concatenate([jnp.sum(grad_in, axis=0), base_rows], axis=0), "replica")
    own_stats = own_stats + swap(own_stats, "tensor", 1)
    own_stats, own_parts = lax.optimization_barrier((own_stats, own_parts))
    own = sum(own_parts)
    own_grad = own[:piece_rows]
    base = lax.all_gather(own[piece_rows:], "shards", axis=0, tiled=True)
    gradient = spread(own_grad, "shards").reshape(row_count, col_count)

    old_factors, own = lax.optimization_barrier((old_factors, own))
    old_block = fold_one(lax.dynamic_slice_in_dim(old_factors, shard, 1, 0))
    own_stats = sum(exchange(own_stats, "replica"))
    own_stats = own_stats + swap(own_stats, "tensor", 2)
    blended = decay_rate * old_block + ((1.0 - decay_rate) / sample_count) * own_stats
    row_of_y = jnp.stack([blended] + [swap(blended, "shards", j) for j in range(1, side)])
    folded = [row_of_y] + [swap(row_of_y, "shards", k * side) for k in range(1, side)]

    positions = jnp.arange(block_count, dtype=jnp.int32)
    earlier = (block_owner[:, None] == block_owner[None, :]) & (
        positions[None, :] < positions[:, None]
    )
    slots = block_owner * capacity + jnp.sum(earlier.astype(jnp.int32), axis=1)
    own_slots = shard * capacity + jnp.arange(capacity, dtype=jnp.int32)
    holds = jnp.max(jnp.where(slots[None, :] == own_slots[:, None], positions[None, :], -1), axis=1)
    right_first = left_count + lax.axis_index("tensor") * right_count
    places = jnp.concatenate([coords, right_first.reshape(1).astype(jnp.int32), holds])
    precond, owned_blocks, align = update(places, folded, gradient, capacity)
    align, base = lax.optimization_barrier((align, base))
    align = align + swap(align, "tensor", 1)
    align = align + swap(align, "tensor", 2)
    clip_scale = jnp.minimum(1.0, clip_norm / jnp.sqrt(align[0, 0]))
    first_row = (shard * replica_count + replica) * own_rows
    own_precond = lax.dynamic_slice_in_dim(precond, first_row, own_rows, 0)
    momentum_next = momentum_rate * momentum + clip_scale * own_precond
    weights_next = base - (step_rate * clip_scale) * precond
    return (weights_next, momentum_next, owned_blocks)


def solution(mesh):
    placed = (
        P(("shards", "tensor", "replica"), None),
        P(("shards", "tensor", "replica"), None),
        P(("shards", "replica"), None, "tensor"),
        P(),
        P(),
        P(("shards", "replica"), "tensor"),
        P(("shards", "replica"), "tensor"),
    )
    return jax.shard_map(
        body,
        mesh=mesh,
        in_specs=placed,
        out_specs=(P(None, "tensor"), P(("shards", "replica"), "tensor"), P("shards", None, None)),
        check_vma=False,
    )
```

```python
import jax
import jax.numpy as jnp
from jax import lax
from jax.experimental import pallas as pl
from jax.experimental.pallas import tpu as pltpu
from jax.sharding import PartitionSpec as P

NS_STEPS = 4


exact_mode = lax.Precision.HIGHEST
decay_rate = 0.75
damping = 0.1
damp_shift = 0.001
clip_norm = 256.0
momentum_rate = 0.9
step_rate = 0.05


def sample_stats(samples, block_size):
    sample_rows, width = samples.shape
    blocks = samples.reshape(sample_rows, width // block_size, block_size)
    return jnp.einsum("tnb,tnc->nbc", blocks, blocks, preferred_element_type=jnp.float32)


def fold_block(block, rows):
    size = block.shape[1]
    half = size // 2
    row = lax.broadcasted_iota(jnp.int32, (half, size), 0)
    col = lax.broadcasted_iota(jnp.int32, (half, size), 1)
    top, bottom = block[:half], block[half:]
    triangle = jnp.where(col >= row, top, pltpu.roll(bottom, half, 1))
    diagonal = jnp.sum(jnp.where(col == row + half, bottom, 0.0), axis=0, keepdims=True)
    return triangle, jnp.broadcast_to(diagonal, (rows - half, size))


def fold_kernel(place_ref, left_ref, right_ref, *folded_refs):
    left_count, size, _ = left_ref.shape
    side = len(folded_refs)
    rows = folded_refs[0].shape[1]
    for k in range(side):
        for j in range(side):
            n = (place_ref[0] ^ k) * side + (place_ref[1] ^ j)
            at = n % left_count
            triangle, diagonal = fold_block(
                jnp.where(n < left_count, left_ref[at], right_ref[at]), rows
            )
            folded_refs[k][j, : size // 2, :] = triangle
            folded_refs[k][j, size // 2 :, :] = diagonal


def fold(places, left_stats, right_stats, side):
    size = left_stats.shape[1]
    return pl.pallas_call(
        fold_kernel,
        in_specs=[
            pl.BlockSpec(memory_space=pltpu.SMEM),
            pl.BlockSpec(memory_space=pltpu.VMEM),
            pl.BlockSpec(memory_space=pltpu.VMEM),
        ],
        out_shape=[jax.ShapeDtypeStruct((side, size // 2 + 8, size), jnp.float32)] * side,
        name="fold",
    )(places, left_stats, right_stats)


def fold_one_kernel(block_ref, folded_ref):
    half = block_ref.shape[1] // 2
    triangle, diagonal = fold_block(block_ref[0], folded_ref.shape[0])
    folded_ref[:half, :] = triangle
    folded_ref[half:, :] = diagonal


def fold_one(block):
    size = block.shape[2]
    return pl.pallas_call(
        fold_one_kernel,
        out_shape=jax.ShapeDtypeStruct((size // 2 + 8, size), jnp.float32),
        name="fold_one",
    )(block)


def dot(a, b):
    return jnp.dot(a, b, precision=exact_mode, preferred_element_type=jnp.float32)


def unfold(part, diagonal):
    half, size = part.shape
    row = lax.broadcasted_iota(jnp.int32, (half, size), 0)
    col = lax.broadcasted_iota(jnp.int32, (half, size), 1)
    turned = jnp.concatenate([part, jnp.zeros_like(part)], axis=0).T
    top = jnp.where(col >= row, part, turned[:half])
    corner = jnp.where(
        col < row + half, pltpu.roll(part, half, 1), pltpu.roll(turned[:half], half, 1)
    )
    corner = jnp.where(col == row + half, diagonal, corner)
    bottom = jnp.where(col < half, turned[half:], corner)
    return jnp.concatenate([top, bottom], axis=0)


def update_kernel(side, place_ref, *refs):
    folded_refs = refs[:side]
    grad_ref, precond_ref, owned_ref, align_ref, blended_ref = refs[side:]
    size = blended_ref.shape[2]
    half = blended_ref.shape[1] - 8
    right_count = grad_ref.shape[1] // size
    left_count = grad_ref.shape[0] // size
    for k in range(side):
        for j in range(side):
            n = (place_ref[0] ^ k) * side + (place_ref[1] ^ j)
            blended_ref[n] = folded_refs[k][j]

    def load(block):
        return unfold(blended_ref[block, :half, :], blended_ref[block, half : half + 1, :])

    on_diagonal = lax.broadcasted_iota(jnp.int32, (size, size), 0) == lax.broadcasted_iota(
        jnp.int32, (size, size), 1
    )
    unit = jnp.where(on_diagonal, 1.0, 0.0)
    powers, bounds, inverses = [], [], []
    for block in list(range(left_count)) + [place_ref[2] + n for n in range(right_count)]:
        mixed = load(block)
        trace = jnp.sum(jnp.where(on_diagonal, mixed, 0.0), keepdims=True)
        damped = mixed + jnp.where(on_diagonal, damping * trace / size + damp_shift, 0.0)
        bound = jnp.max(jnp.sum(jnp.abs(damped), axis=1, keepdims=True), keepdims=True)
        power = unit - damped / bound
        powers.append(power)
        bounds.append(bound)
        inverses.append(unit + power)
    for step in range(NS_STEPS - 1):
        powers = [dot(power, power) for power in powers]
        inverses = [x + dot(x, power) for x, power in zip(inverses, powers)]
    inverses = [x / bound for x, bound in zip(inverses, bounds)]

    total = jnp.zeros((size, size), jnp.float32)
    for a in range(left_count):
        rows = slice(a * size, (a + 1) * size)
        left_part = dot(inverses[a], grad_ref[rows, :])
        for c in range(right_count):
            cols = slice(c * size, (c + 1) * size)
            value = dot(left_part[:, cols], inverses[left_count + c])
            precond_ref[rows, cols] = value
            total = total + value * grad_ref[rows, cols]
    align_ref[...] = jnp.broadcast_to(jnp.sum(total, keepdims=True), align_ref.shape)

    for place in range(owned_ref.shape[0]):
        block = place_ref[3 + place]
        value = load(jnp.maximum(block, 0))
        owned_ref[place] = jnp.where(block >= 0, value, jnp.zeros_like(value))


def update(places, folded, gradient, capacity):
    side, rows, size = folded[0].shape
    return pl.pallas_call(
        lambda *refs: update_kernel(side, *refs),
        in_specs=[pl.BlockSpec(memory_space=pltpu.SMEM)]
        + [pl.BlockSpec(memory_space=pltpu.VMEM)] * (side + 1),
        out_shape=(
            jax.ShapeDtypeStruct(gradient.shape, jnp.float32),
            jax.ShapeDtypeStruct((capacity, size, size), jnp.float32),
            jax.ShapeDtypeStruct((1, size), jnp.float32),
        ),
        scratch_shapes=[pltpu.VMEM((side * side, rows, size), jnp.float32)],
        compiler_params=pltpu.CompilerParams(vmem_limit_bytes=40 * 1024 * 1024),
        name="update",
    )(places, *folded, gradient)


def finish_kernel(row_ref, align_ref, momentum_ref, precond_ref, base_ref, weights_ref, next_ref):
    scale = jnp.minimum(1.0, clip_norm / jnp.sqrt(align_ref[0:1, 0:1]))
    rows = next_ref.shape[0]
    own = precond_ref[pl.ds(pl.multiple_of(row_ref[0], rows), rows), :]
    next_ref[...] = momentum_rate * momentum_ref[...] + scale * own
    weights_ref[...] = base_ref[...] - (step_rate * scale) * precond_ref[...]


def finish(first_row, align, momentum, precond, base):
    return pl.pallas_call(
        finish_kernel,
        in_specs=[pl.BlockSpec(memory_space=pltpu.SMEM)]
        + [pl.BlockSpec(memory_space=pltpu.VMEM)] * 4,
        out_shape=(
            jax.ShapeDtypeStruct(base.shape, jnp.float32),
            jax.ShapeDtypeStruct(momentum.shape, jnp.float32),
        ),
        name="finish",
    )(first_row.reshape(1).astype(jnp.int32), align, momentum, precond, base)


def after(value, first):
    return lax.optimization_barrier((value, first))[0]


def swap(value, axis, flip):
    size = lax.axis_size(axis)
    return lax.ppermute(value, axis, [(i, i ^ flip) for i in range(size)])


def exchange(value, axis):
    return [value] + [swap(value, axis, flip) for flip in range(1, lax.axis_size(axis))]


def spread(value, axis):
    copies = jnp.broadcast_to(value[None], (lax.axis_size(axis),) + value.shape)
    return lax.all_to_all(copies, axis, 0, 0)


def body(activations, grads_out, grad_parts, old_factors, block_owner, weights, momentum):
    shard_count = lax.axis_size("shards")
    replica_count = lax.axis_size("replica")
    block_count = old_factors.shape[0]
    block_size = old_factors.shape[1]
    capacity = (block_count + shard_count - 1) // shard_count + 1
    sample_count = activations.shape[0] * shard_count * lax.axis_size("tensor") * replica_count
    partial_grad = grad_parts[0]
    row_count, col_count = partial_grad.shape
    left_count = row_count // block_size
    right_count = col_count // block_size
    piece_rows = row_count // shard_count
    own_rows = weights.shape[0]
    shard = lax.axis_index("shards")
    replica = lax.axis_index("replica")

    grad_in = lax.all_to_all(partial_grad.reshape(shard_count, piece_rows, col_count), "shards", 0, 0)

    side = 4
    coords = jnp.stack([shard // side, shard % side]).astype(jnp.int32)
    along_x = fold(
        coords,
        sample_stats(activations, block_size),
        sample_stats(grads_out, block_size),
        side,
    )
    parts = [along_x[0]] + [swap(along_x[k], "shards", k * side) for k in range(1, side)]
    along_y = [sum(part[j] for part in parts) for j in range(side)]
    own_stats = along_y[0] + sum(swap(along_y[j], "shards", j) for j in range(1, side))
    own_stats = own_stats + swap(own_stats, "tensor", 1)

    weights, momentum_then, old_then = after((weights, momentum, old_factors), along_x[0])
    base_parts = exchange(weights - (step_rate * momentum_rate) * momentum_then, "replica")
    base_rows = []
    for place in range(replica_count):
        rows = base_parts[0]
        for flip in range(1, replica_count):
            rows = jnp.where(replica ^ flip == place, base_parts[flip], rows)
        base_rows.append(rows)
    base = lax.all_gather(jnp.concatenate(base_rows, axis=0), "shards", axis=0, tiled=True)
    old_block = fold_one(lax.dynamic_slice_in_dim(old_then, shard, 1, 0))

    grad_parts_in = exchange(jnp.sum(after(grad_in, along_x[0]), axis=0), "replica")
    own_grad = sum(after(grad_parts_in, own_stats))
    gradient = spread(own_grad, "shards").reshape(row_count, col_count)

    own_stats = sum(exchange(after(own_stats, old_block), "replica"))
    own_stats = own_stats + swap(own_stats, "tensor", 2)
    blended = decay_rate * old_block + ((1.0 - decay_rate) / sample_count) * own_stats
    row_of_y = jnp.stack([blended] + [swap(blended, "shards", j) for j in range(1, side)])
    folded = [row_of_y] + [swap(row_of_y, "shards", k * side) for k in range(1, side)]

    positions = jnp.arange(block_count, dtype=jnp.int32)
    earlier = (block_owner[:, None] == block_owner[None, :]) & (
        positions[None, :] < positions[:, None]
    )
    slots = block_owner * capacity + jnp.sum(earlier.astype(jnp.int32), axis=1)
    own_slots = shard * capacity + jnp.arange(capacity, dtype=jnp.int32)
    holds = jnp.max(jnp.where(slots[None, :] == own_slots[:, None], positions[None, :], -1), axis=1)
    right_first = left_count + lax.axis_index("tensor") * right_count
    places = jnp.concatenate([coords, right_first.reshape(1).astype(jnp.int32), holds])
    precond, owned_blocks, align = update(places, folded, gradient, capacity)
    align, base = lax.optimization_barrier((align, base))
    align = align + swap(align, "tensor", 1)
    align = align + swap(align, "tensor", 2)
    first_row = (shard * replica_count + replica) * own_rows
    weights_next, momentum_next = finish(first_row, align, momentum, precond, base)
    return (weights_next, momentum_next, owned_blocks)


def solution(mesh):
    placed = (
        P(("shards", "tensor", "replica"), None),
        P(("shards", "tensor", "replica"), None),
        P(("shards", "replica"), None, "tensor"),
        P(),
        P(),
        P(("shards", "replica"), "tensor"),
        P(("shards", "replica"), "tensor"),
    )
    return jax.shard_map(
        body,
        mesh=mesh,
        in_specs=placed,
        out_specs=(P(None, "tensor"), P(("shards", "replica"), "tensor"), P("shards", None, None)),
        check_vma=False,
    )
```

```python
import jax
import jax.numpy as jnp
from jax import lax
from jax.experimental import pallas as pl
from jax.experimental.pallas import tpu as pltpu
from jax.sharding import PartitionSpec as P

NS_STEPS = 4


exact_mode = lax.Precision.HIGHEST
decay_rate = 0.75
damping = 0.1
damp_shift = 0.001
clip_norm = 256.0
momentum_rate = 0.9
step_rate = 0.05


def sample_stats(samples, block_size):
    sample_rows, width = samples.shape
    blocks = samples.reshape(sample_rows, width // block_size, block_size)
    return jnp.einsum("tnb,tnc->nbc", blocks, blocks, preferred_element_type=jnp.float32)


def fold_block(block, rows):
    size = block.shape[1]
    half = size // 2
    row = lax.broadcasted_iota(jnp.int32, (half, size), 0)
    col = lax.broadcasted_iota(jnp.int32, (half, size), 1)
    top, bottom = block[:half], block[half:]
    triangle = jnp.where(col >= row, top, pltpu.roll(bottom, half, 1))
    diagonal = jnp.sum(jnp.where(col == row + half, bottom, 0.0), axis=0, keepdims=True)
    return triangle, jnp.broadcast_to(diagonal, (rows - half, size))


def fold_kernel(place_ref, left_ref, right_ref, *folded_refs):
    left_count, size, _ = left_ref.shape
    side = len(folded_refs)
    rows = folded_refs[0].shape[1]
    for k in range(side):
        for j in range(side):
            n = (place_ref[0] ^ k) * side + (place_ref[1] ^ j)
            at = n % left_count
            triangle, diagonal = fold_block(
                jnp.where(n < left_count, left_ref[at], right_ref[at]), rows
            )
            folded_refs[k][j, : size // 2, :] = triangle
            folded_refs[k][j, size // 2 :, :] = diagonal


def fold(places, left_stats, right_stats, side):
    size = left_stats.shape[1]
    return pl.pallas_call(
        fold_kernel,
        in_specs=[
            pl.BlockSpec(memory_space=pltpu.SMEM),
            pl.BlockSpec(memory_space=pltpu.VMEM),
            pl.BlockSpec(memory_space=pltpu.VMEM),
        ],
        out_shape=[jax.ShapeDtypeStruct((side, size // 2 + 8, size), jnp.float32)] * side,
        name="fold",
    )(places, left_stats, right_stats)


def fold_one_kernel(block_ref, folded_ref):
    half = block_ref.shape[1] // 2
    triangle, diagonal = fold_block(block_ref[0], folded_ref.shape[0])
    folded_ref[:half, :] = triangle
    folded_ref[half:, :] = diagonal


def fold_one(block):
    size = block.shape[2]
    return pl.pallas_call(
        fold_one_kernel,
        out_shape=jax.ShapeDtypeStruct((size // 2 + 8, size), jnp.float32),
        name="fold_one",
    )(block)


def dot(a, b):
    return jnp.dot(a, b, precision=exact_mode, preferred_element_type=jnp.float32)


def unfold(part, diagonal):
    half, size = part.shape
    row = lax.broadcasted_iota(jnp.int32, (half, size), 0)
    col = lax.broadcasted_iota(jnp.int32, (half, size), 1)
    turned = jnp.concatenate([part, jnp.zeros_like(part)], axis=0).T
    top = jnp.where(col >= row, part, turned[:half])
    corner = jnp.where(
        col < row + half, pltpu.roll(part, half, 1), pltpu.roll(turned[:half], half, 1)
    )
    corner = jnp.where(col == row + half, diagonal, corner)
    bottom = jnp.where(col < half, turned[half:], corner)
    return jnp.concatenate([top, bottom], axis=0)


def update_kernel(side, place_ref, *refs):
    folded_refs = refs[:side]
    grad_ref, precond_ref, owned_ref, align_ref, blended_ref = refs[side:]
    size = blended_ref.shape[2]
    half = blended_ref.shape[1] - 8
    right_count = grad_ref.shape[1] // size
    left_count = grad_ref.shape[0] // size
    for k in range(side):
        for j in range(side):
            n = (place_ref[0] ^ k) * side + (place_ref[1] ^ j)
            blended_ref[n] = folded_refs[k][j]

    def load(block):
        return unfold(blended_ref[block, :half, :], blended_ref[block, half : half + 1, :])

    on_diagonal = lax.broadcasted_iota(jnp.int32, (size, size), 0) == lax.broadcasted_iota(
        jnp.int32, (size, size), 1
    )
    unit = jnp.where(on_diagonal, 1.0, 0.0)
    powers, bounds, inverses = [], [], []
    for block in list(range(left_count)) + [place_ref[2] + n for n in range(right_count)]:
        mixed = load(block)
        trace = jnp.sum(jnp.where(on_diagonal, mixed, 0.0), keepdims=True)
        damped = mixed + jnp.where(on_diagonal, damping * trace / size + damp_shift, 0.0)
        bound = jnp.max(jnp.sum(jnp.abs(damped), axis=1, keepdims=True), keepdims=True)
        power = unit - damped / bound
        powers.append(power)
        bounds.append(bound)
        inverses.append(unit + power)
    for step in range(NS_STEPS - 1):
        powers = [dot(power, power) for power in powers]
        inverses = [x + dot(x, power) for x, power in zip(inverses, powers)]
    inverses = [x / bound for x, bound in zip(inverses, bounds)]

    total = jnp.zeros((size, size), jnp.float32)
    for a in range(left_count):
        rows = slice(a * size, (a + 1) * size)
        left_part = dot(inverses[a], grad_ref[rows, :])
        for c in range(right_count):
            cols = slice(c * size, (c + 1) * size)
            value = dot(left_part[:, cols], inverses[left_count + c])
            precond_ref[rows, cols] = value
            total = total + value * grad_ref[rows, cols]
    align_ref[...] = jnp.broadcast_to(jnp.sum(total, keepdims=True), align_ref.shape)

    for place in range(owned_ref.shape[0]):
        block = place_ref[3 + place]
        value = load(jnp.maximum(block, 0))
        owned_ref[place] = jnp.where(block >= 0, value, jnp.zeros_like(value))


def update(places, folded, gradient, capacity):
    side, rows, size = folded[0].shape
    return pl.pallas_call(
        lambda *refs: update_kernel(side, *refs),
        in_specs=[pl.BlockSpec(memory_space=pltpu.SMEM)]
        + [pl.BlockSpec(memory_space=pltpu.VMEM)] * (side + 1),
        out_shape=(
            jax.ShapeDtypeStruct(gradient.shape, jnp.float32),
            jax.ShapeDtypeStruct((capacity, size, size), jnp.float32),
            jax.ShapeDtypeStruct((1, size), jnp.float32),
        ),
        scratch_shapes=[pltpu.VMEM((side * side, rows, size), jnp.float32)],
        compiler_params=pltpu.CompilerParams(vmem_limit_bytes=40 * 1024 * 1024),
        name="update",
    )(places, *folded, gradient)


def finish_kernel(row_ref, align_ref, momentum_ref, precond_ref, base_ref, weights_ref, next_ref):
    scale = jnp.minimum(1.0, clip_norm / jnp.sqrt(align_ref[0:1, 0:1]))
    rows = next_ref.shape[0]
    own = precond_ref[pl.ds(pl.multiple_of(row_ref[0], rows), rows), :]
    next_ref[...] = momentum_rate * momentum_ref[...] + scale * own
    weights_ref[...] = base_ref[...] - (step_rate * scale) * precond_ref[...]


def finish(first_row, align, momentum, precond, base):
    return pl.pallas_call(
        finish_kernel,
        in_specs=[pl.BlockSpec(memory_space=pltpu.SMEM)]
        + [pl.BlockSpec(memory_space=pltpu.VMEM)] * 4,
        out_shape=(
            jax.ShapeDtypeStruct(base.shape, jnp.float32),
            jax.ShapeDtypeStruct(momentum.shape, jnp.float32),
        ),
        name="finish",
    )(first_row.reshape(1).astype(jnp.int32), align, momentum, precond, base)


def after(value, first):
    return lax.optimization_barrier((value, first))[0]


def swap(value, axis, flip):
    size = lax.axis_size(axis)
    return lax.ppermute(value, axis, [(i, i ^ flip) for i in range(size)])


def exchange(value, axis):
    return [value] + [swap(value, axis, flip) for flip in range(1, lax.axis_size(axis))]


def spread(value, axis):
    copies = jnp.broadcast_to(value[None], (lax.axis_size(axis),) + value.shape)
    return lax.all_to_all(copies, axis, 0, 0)


def body(activations, grads_out, grad_parts, old_factors, block_owner, weights, momentum):
    shard_count = lax.axis_size("shards")
    replica_count = lax.axis_size("replica")
    block_count = old_factors.shape[0]
    block_size = old_factors.shape[1]
    capacity = (block_count + shard_count - 1) // shard_count + 1
    sample_count = activations.shape[0] * shard_count * lax.axis_size("tensor") * replica_count
    partial_grad = grad_parts[0]
    row_count, col_count = partial_grad.shape
    left_count = row_count // block_size
    right_count = col_count // block_size
    piece_rows = row_count // shard_count
    own_rows = weights.shape[0]
    shard = lax.axis_index("shards")
    replica = lax.axis_index("replica")

    grad_in = lax.all_to_all(partial_grad.reshape(shard_count, piece_rows, col_count), "shards", 0, 0)

    side = 4
    coords = jnp.stack([shard // side, shard % side]).astype(jnp.int32)
    along_x = fold(
        coords,
        sample_stats(activations, block_size),
        sample_stats(grads_out, block_size),
        side,
    )
    parts = [along_x[0]] + [swap(along_x[k], "shards", k * side) for k in range(1, side)]

    grad_in, weights, momentum_then, old_then = after(
        (grad_in, weights, momentum, old_factors), along_x[0]
    )
    old_block = fold_one(lax.dynamic_slice_in_dim(old_then, shard, 1, 0))
    base_parts = exchange(weights - (step_rate * momentum_rate) * momentum_then, "replica")
    base_rows = []
    for place in range(replica_count):
        rows = base_parts[0]
        for flip in range(1, replica_count):
            rows = jnp.where(replica ^ flip == place, base_parts[flip], rows)
        base_rows.append(rows)
    base = lax.all_gather(jnp.concatenate(base_rows, axis=0), "shards", axis=0, tiled=True)
    grad_rows = jnp.sum(grad_in, axis=0)
    row_parts = exchange(grad_rows, "replica")

    parts = after(parts, (grad_rows, old_block))
    along_y = [sum(part[j] for part in parts) for j in range(side)]
    own_stats = along_y[0] + sum(swap(along_y[j], "shards", j) for j in range(1, side))
    own_stats = own_stats + swap(own_stats, "tensor", 1)

    own_grad = sum(after(row_parts, own_stats))
    gradient = spread(own_grad, "shards").reshape(row_count, col_count)

    own_stats = sum(exchange(own_stats, "replica"))
    own_stats = own_stats + swap(own_stats, "tensor", 2)
    blended = decay_rate * old_block + ((1.0 - decay_rate) / sample_count) * own_stats
    row_of_y = jnp.stack([blended] + [swap(blended, "shards", j) for j in range(1, side)])
    folded = [row_of_y] + [swap(row_of_y, "shards", k * side) for k in range(1, side)]

    positions = jnp.arange(block_count, dtype=jnp.int32)
    earlier = (block_owner[:, None] == block_owner[None, :]) & (
        positions[None, :] < positions[:, None]
    )
    slots = block_owner * capacity + jnp.sum(earlier.astype(jnp.int32), axis=1)
    own_slots = shard * capacity + jnp.arange(capacity, dtype=jnp.int32)
    holds = jnp.max(jnp.where(slots[None, :] == own_slots[:, None], positions[None, :], -1), axis=1)
    right_first = left_count + lax.axis_index("tensor") * right_count
    places = jnp.concatenate([coords, right_first.reshape(1).astype(jnp.int32), holds])
    precond, owned_blocks, align = update(places, folded, gradient, capacity)
    align, base = lax.optimization_barrier((align, base))
    align = align + swap(align, "tensor", 1)
    align = align + swap(align, "tensor", 2)
    first_row = (shard * replica_count + replica) * own_rows
    weights_next, momentum_next = finish(first_row, align, momentum, precond, base)
    return (weights_next, momentum_next, owned_blocks)


def solution(mesh):
    placed = (
        P(("shards", "tensor", "replica"), None),
        P(("shards", "tensor", "replica"), None),
        P(("shards", "replica"), None, "tensor"),
        P(),
        P(),
        P(("shards", "replica"), "tensor"),
        P(("shards", "replica"), "tensor"),
    )
    return jax.shard_map(
        body,
        mesh=mesh,
        in_specs=placed,
        out_specs=(P(None, "tensor"), P(("shards", "replica"), "tensor"), P("shards", None, None)),
        check_vma=False,
    )
```

```python
import jax
import jax.numpy as jnp
from jax import lax
from jax.experimental import pallas as pl
from jax.experimental.pallas import tpu as pltpu
from jax.sharding import PartitionSpec as P

NS_STEPS = 4


exact_mode = lax.Precision.HIGHEST
decay_rate = 0.75
damping = 0.1
damp_shift = 0.001
clip_norm = 256.0
momentum_rate = 0.9
step_rate = 0.05


def sample_stats(samples, block_size):
    sample_rows, width = samples.shape
    blocks = samples.reshape(sample_rows, width // block_size, block_size)
    return jnp.einsum("tnb,tnc->nbc", blocks, blocks, preferred_element_type=jnp.float32)


def fold_block(block, rows):
    size = block.shape[1]
    half = size // 2
    row = lax.broadcasted_iota(jnp.int32, (half, size), 0)
    col = lax.broadcasted_iota(jnp.int32, (half, size), 1)
    top, bottom = block[:half], block[half:]
    triangle = jnp.where(col >= row, top, pltpu.roll(bottom, half, 1))
    diagonal = jnp.sum(jnp.where(col == row + half, bottom, 0.0), axis=0, keepdims=True)
    return triangle, jnp.broadcast_to(diagonal, (rows - half, size))


def fold_kernel(left_ref, right_ref, folded_ref):
    left_count, size, _ = left_ref.shape
    for n in range(folded_ref.shape[0]):
        block = left_ref[n] if n < left_count else right_ref[n - left_count]
        triangle, diagonal = fold_block(block, folded_ref.shape[1])
        folded_ref[n, : size // 2, :] = triangle
        folded_ref[n, size // 2 :, :] = diagonal


def fold(left_stats, right_stats):
    count, size, _ = left_stats.shape
    return pl.pallas_call(
        fold_kernel,
        out_shape=jax.ShapeDtypeStruct(
            (count + right_stats.shape[0], size // 2 + 8, size), jnp.float32
        ),
        name="fold",
    )(left_stats, right_stats)


def fold_one_kernel(block_ref, folded_ref):
    half = block_ref.shape[1] // 2
    triangle, diagonal = fold_block(block_ref[0], folded_ref.shape[0])
    folded_ref[:half, :] = triangle
    folded_ref[half:, :] = diagonal


def fold_one(block):
    size = block.shape[2]
    return pl.pallas_call(
        fold_one_kernel,
        out_shape=jax.ShapeDtypeStruct((size // 2 + 8, size), jnp.float32),
        name="fold_one",
    )(block)


def dot(a, b):
    return jnp.dot(a, b, precision=exact_mode, preferred_element_type=jnp.float32)


def unfold(part, diagonal):
    half, size = part.shape
    row = lax.broadcasted_iota(jnp.int32, (half, size), 0)
    col = lax.broadcasted_iota(jnp.int32, (half, size), 1)
    turned = jnp.concatenate([part, jnp.zeros_like(part)], axis=0).T
    top = jnp.where(col >= row, part, turned[:half])
    corner = jnp.where(
        col < row + half, pltpu.roll(part, half, 1), pltpu.roll(turned[:half], half, 1)
    )
    corner = jnp.where(col == row + half, diagonal, corner)
    bottom = jnp.where(col < half, turned[half:], corner)
    return jnp.concatenate([top, bottom], axis=0)


def update_kernel(place_ref, folded_ref, grad_ref, precond_ref, owned_ref, align_ref):
    size = folded_ref.shape[2]
    half = size // 2
    right_count = grad_ref.shape[1] // size
    left_count = grad_ref.shape[0] // size

    def load(block):
        return unfold(folded_ref[block, :half, :], folded_ref[block, half : half + 1, :])

    on_diagonal = lax.broadcasted_iota(jnp.int32, (size, size), 0) == lax.broadcasted_iota(
        jnp.int32, (size, size), 1
    )
    unit = jnp.where(on_diagonal, 1.0, 0.0)
    powers, bounds, inverses = [], [], []
    for block in list(range(left_count)) + [place_ref[0] + n for n in range(right_count)]:
        mixed = load(block)
        trace = jnp.sum(jnp.where(on_diagonal, mixed, 0.0), keepdims=True)
        damped = mixed + jnp.where(on_diagonal, damping * trace / size + damp_shift, 0.0)
        bound = jnp.max(jnp.sum(jnp.abs(damped), axis=1, keepdims=True), keepdims=True)
        power = unit - damped / bound
        powers.append(power)
        bounds.append(bound)
        inverses.append(unit + power)
    for step in range(NS_STEPS - 1):
        powers = [dot(power, power) for power in powers]
        inverses = [x + dot(x, power) for x, power in zip(inverses, powers)]
    inverses = [x / bound for x, bound in zip(inverses, bounds)]

    total = jnp.zeros((size, size), jnp.float32)
    for a in range(left_count):
        rows = slice(a * size, (a + 1) * size)
        left_part = dot(inverses[a], grad_ref[rows, :])
        for c in range(right_count):
            cols = slice(c * size, (c + 1) * size)
            value = dot(left_part[:, cols], inverses[left_count + c])
            precond_ref[rows, cols] = value
            total = total + value * grad_ref[rows, cols]
    align_ref[...] = jnp.broadcast_to(jnp.sum(total, keepdims=True), align_ref.shape)

    for place in range(owned_ref.shape[0]):
        block = place_ref[1 + place]
        value = load(jnp.maximum(block, 0))
        owned_ref[place] = jnp.where(block >= 0, value, jnp.zeros_like(value))


def update(places, folded, gradient, capacity):
    size = folded.shape[2]
    return pl.pallas_call(
        update_kernel,
        in_specs=[
            pl.BlockSpec(memory_space=pltpu.SMEM),
            pl.BlockSpec(memory_space=pltpu.VMEM),
            pl.BlockSpec(memory_space=pltpu.VMEM),
        ],
        out_shape=(
            jax.ShapeDtypeStruct(gradient.shape, jnp.float32),
            jax.ShapeDtypeStruct((capacity, size, size), jnp.float32),
            jax.ShapeDtypeStruct((1, size), jnp.float32),
        ),
        compiler_params=pltpu.CompilerParams(vmem_limit_bytes=40 * 1024 * 1024),
        name="update",
    )(places, folded, gradient)


def finish_kernel(row_ref, align_ref, momentum_ref, precond_ref, base_ref, weights_ref, next_ref):
    scale = jnp.minimum(1.0, clip_norm / jnp.sqrt(align_ref[0:1, 0:1]))
    rows = next_ref.shape[0]
    own = precond_ref[pl.ds(pl.multiple_of(row_ref[0], rows), rows), :]
    next_ref[...] = momentum_rate * momentum_ref[...] + scale * own
    weights_ref[...] = base_ref[...] - (step_rate * scale) * precond_ref[...]


def finish(first_row, align, momentum, precond, base):
    return pl.pallas_call(
        finish_kernel,
        in_specs=[pl.BlockSpec(memory_space=pltpu.SMEM)]
        + [pl.BlockSpec(memory_space=pltpu.VMEM)] * 4,
        out_shape=(
            jax.ShapeDtypeStruct(base.shape, jnp.float32),
            jax.ShapeDtypeStruct(momentum.shape, jnp.float32),
        ),
        name="finish",
    )(first_row.reshape(1).astype(jnp.int32), align, momentum, precond, base)


def after(value, first):
    return lax.optimization_barrier((value, first))[0]


def swap(value, axis, flip):
    size = lax.axis_size(axis)
    return lax.ppermute(value, axis, [(i, i ^ flip) for i in range(size)])


def exchange(value, axis):
    return [value] + [swap(value, axis, flip) for flip in range(1, lax.axis_size(axis))]


def spread(value, axis):
    copies = jnp.broadcast_to(value[None], (lax.axis_size(axis),) + value.shape)
    return lax.all_to_all(copies, axis, 0, 0)


def body(activations, grads_out, grad_parts, old_factors, block_owner, weights, momentum):
    shard_count = lax.axis_size("shards")
    replica_count = lax.axis_size("replica")
    block_count = old_factors.shape[0]
    block_size = old_factors.shape[1]
    capacity = (block_count + shard_count - 1) // shard_count + 1
    sample_count = activations.shape[0] * shard_count * lax.axis_size("tensor") * replica_count
    partial_grad = grad_parts[0]
    row_count, col_count = partial_grad.shape
    left_count = row_count // block_size
    right_count = col_count // block_size
    piece_rows = row_count // shard_count
    own_rows = weights.shape[0]
    shard = lax.axis_index("shards")
    replica = lax.axis_index("replica")

    grad_in = lax.all_to_all(partial_grad.reshape(shard_count, piece_rows, col_count), "shards", 0, 0)

    folded = fold(sample_stats(activations, block_size), sample_stats(grads_out, block_size))
    folded, grad_in = lax.optimization_barrier((folded, grad_in))
    stats_in = lax.all_to_all(folded, "shards", 0, 0)

    base = weights - (step_rate * momentum_rate) * momentum
    base_rows = lax.dynamic_update_slice_in_dim(
        jnp.zeros((piece_rows, col_count), jnp.float32), base, replica * own_rows, 0
    )
    grad_rows = jnp.sum(grad_in, axis=0)
    rows = sum(exchange(jnp.concatenate([grad_rows, base_rows], axis=0), "replica"))
    base = lax.all_gather(rows[piece_rows:], "shards", axis=0, tiled=True)

    old_block = fold_one(lax.dynamic_slice_in_dim(after(old_factors, rows), shard, 1, 0))
    own_stats = jnp.sum(stats_in, axis=0)
    own_stats, own_grad, old_block = lax.optimization_barrier(
        (own_stats, rows[:piece_rows], old_block)
    )
    gradient = spread(own_grad, "shards").reshape(row_count, col_count)
    own_stats = own_stats + swap(own_stats, "tensor", 1)
    own_stats = sum(exchange(own_stats, "replica"))
    own_stats = own_stats + swap(own_stats, "tensor", 2)
    blended = decay_rate * old_block + ((1.0 - decay_rate) / sample_count) * own_stats
    folded = spread(after(blended, gradient), "shards")

    positions = jnp.arange(block_count, dtype=jnp.int32)
    earlier = (block_owner[:, None] == block_owner[None, :]) & (
        positions[None, :] < positions[:, None]
    )
    slots = block_owner * capacity + jnp.sum(earlier.astype(jnp.int32), axis=1)
    own_slots = shard * capacity + jnp.arange(capacity, dtype=jnp.int32)
    holds = jnp.max(jnp.where(slots[None, :] == own_slots[:, None], positions[None, :], -1), axis=1)
    right_first = left_count + lax.axis_index("tensor") * right_count
    places = jnp.concatenate([right_first.reshape(1).astype(jnp.int32), holds])
    precond, owned_blocks, align = update(places, folded, gradient, capacity)
    align, base = lax.optimization_barrier((align, base))
    align = align + swap(align, "tensor", 1)
    align = align + swap(align, "tensor", 2)
    first_row = (shard * replica_count + replica) * own_rows
    weights_next, momentum_next = finish(first_row, align, momentum, precond, base)
    return (weights_next, momentum_next, owned_blocks)


def solution(mesh):
    placed = (
        P(("shards", "tensor", "replica"), None),
        P(("shards", "tensor", "replica"), None),
        P(("shards", "replica"), None, "tensor"),
        P(),
        P(),
        P(("shards", "replica"), "tensor"),
        P(("shards", "replica"), "tensor"),
    )
    return jax.shard_map(
        body,
        mesh=mesh,
        in_specs=placed,
        out_specs=(P(None, "tensor"), P(("shards", "replica"), "tensor"), P("shards", None, None)),
        check_vma=False,
    )
```

```python
import jax
import jax.numpy as jnp
from jax import lax
from jax.experimental import pallas as pl
from jax.experimental.pallas import tpu as pltpu
from jax.sharding import PartitionSpec as P

NS_STEPS = 4


exact_mode = lax.Precision.HIGHEST
decay_rate = 0.75
damping = 0.1
damp_shift = 0.001
clip_norm = 256.0
momentum_rate = 0.9
step_rate = 0.05


def sample_stats(samples, block_size):
    sample_rows, width = samples.shape
    blocks = samples.reshape(sample_rows, width // block_size, block_size)
    return jnp.einsum("tnb,tnc->nbc", blocks, blocks, preferred_element_type=jnp.float32)


def fold_block(block, rows):
    size = block.shape[1]
    half = size // 2
    row = lax.broadcasted_iota(jnp.int32, (half, size), 0)
    col = lax.broadcasted_iota(jnp.int32, (half, size), 1)
    top, bottom = block[:half], block[half:]
    triangle = jnp.where(col >= row, top, pltpu.roll(bottom, half, 1))
    diagonal = jnp.sum(jnp.where(col == row + half, bottom, 0.0), axis=0, keepdims=True)
    return triangle, jnp.broadcast_to(diagonal, (rows - half, size))


def fold_kernel(left_ref, right_ref, folded_ref):
    left_count, size, _ = left_ref.shape
    for n in range(folded_ref.shape[0]):
        block = left_ref[n] if n < left_count else right_ref[n - left_count]
        triangle, diagonal = fold_block(block, folded_ref.shape[1])
        folded_ref[n, : size // 2, :] = triangle
        folded_ref[n, size // 2 :, :] = diagonal


def fold(left_stats, right_stats):
    count, size, _ = left_stats.shape
    return pl.pallas_call(
        fold_kernel,
        out_shape=jax.ShapeDtypeStruct(
            (count + right_stats.shape[0], size // 2 + 8, size), jnp.float32
        ),
        name="fold",
    )(left_stats, right_stats)


def fold_one_kernel(block_ref, folded_ref):
    half = block_ref.shape[1] // 2
    triangle, diagonal = fold_block(block_ref[0], folded_ref.shape[0])
    folded_ref[:half, :] = triangle
    folded_ref[half:, :] = diagonal


def fold_one(block):
    size = block.shape[2]
    return pl.pallas_call(
        fold_one_kernel,
        out_shape=jax.ShapeDtypeStruct((size // 2 + 8, size), jnp.float32),
        name="fold_one",
    )(block)


def dot(a, b):
    return jnp.dot(a, b, precision=exact_mode, preferred_element_type=jnp.float32)


def unfold(part, diagonal):
    half, size = part.shape
    row = lax.broadcasted_iota(jnp.int32, (half, size), 0)
    col = lax.broadcasted_iota(jnp.int32, (half, size), 1)
    turned = jnp.concatenate([part, jnp.zeros_like(part)], axis=0).T
    top = jnp.where(col >= row, part, turned[:half])
    corner = jnp.where(
        col < row + half, pltpu.roll(part, half, 1), pltpu.roll(turned[:half], half, 1)
    )
    corner = jnp.where(col == row + half, diagonal, corner)
    bottom = jnp.where(col < half, turned[half:], corner)
    return jnp.concatenate([top, bottom], axis=0)


def inverse_kernel(place_ref, folded_ref, inverse_ref, owned_ref):
    needed, size, _ = inverse_ref.shape
    half = size // 2
    right_count = needed - folded_ref.shape[0] // 2
    left_count = needed - right_count

    def load(block):
        return unfold(folded_ref[block, :half, :], folded_ref[block, half : half + 1, :])

    on_diagonal = lax.broadcasted_iota(jnp.int32, (size, size), 0) == lax.broadcasted_iota(
        jnp.int32, (size, size), 1
    )
    unit = jnp.where(on_diagonal, 1.0, 0.0)
    powers, bounds, inverses = [], [], []
    for block in list(range(left_count)) + [place_ref[0] + n for n in range(right_count)]:
        mixed = load(block)
        trace = jnp.sum(jnp.where(on_diagonal, mixed, 0.0), keepdims=True)
        damped = mixed + jnp.where(on_diagonal, damping * trace / size + damp_shift, 0.0)
        bound = jnp.max(jnp.sum(jnp.abs(damped), axis=1, keepdims=True), keepdims=True)
        power = unit - damped / bound
        powers.append(power)
        bounds.append(bound)
        inverses.append(unit + power)
    for step in range(NS_STEPS - 1):
        powers = [dot(power, power) for power in powers]
        inverses = [x + dot(x, power) for x, power in zip(inverses, powers)]
    for n, (x, bound) in enumerate(zip(inverses, bounds)):
        inverse_ref[n] = x / bound

    for place in range(owned_ref.shape[0]):
        block = place_ref[1 + place]
        value = load(jnp.maximum(block, 0))
        owned_ref[place] = jnp.where(block >= 0, value, jnp.zeros_like(value))


def invert_needed(places, folded, needed, capacity):
    size = folded.shape[2]
    return pl.pallas_call(
        inverse_kernel,
        in_specs=[
            pl.BlockSpec(memory_space=pltpu.SMEM),
            pl.BlockSpec(memory_space=pltpu.VMEM),
        ],
        out_shape=(
            jax.ShapeDtypeStruct((needed, size, size), jnp.float32),
            jax.ShapeDtypeStruct((capacity, size, size), jnp.float32),
        ),
        name="inverse",
    )(places, folded)


def precondition_kernel(inverse_ref, grad_ref, precond_ref, align_ref):
    size = inverse_ref.shape[1]
    left_count = grad_ref.shape[0] // size
    right_count = grad_ref.shape[1] // size
    total = jnp.zeros((size, size), jnp.float32)
    for a in range(left_count):
        rows = slice(a * size, (a + 1) * size)
        left_part = dot(inverse_ref[a], grad_ref[rows, :])
        for c in range(right_count):
            cols = slice(c * size, (c + 1) * size)
            value = dot(left_part[:, cols], inverse_ref[left_count + c])
            precond_ref[rows, cols] = value
            total = total + value * grad_ref[rows, cols]
    align_ref[...] = jnp.broadcast_to(jnp.sum(total, keepdims=True), align_ref.shape)


def precondition(inverses, gradient):
    return pl.pallas_call(
        precondition_kernel,
        out_shape=(
            jax.ShapeDtypeStruct(gradient.shape, jnp.float32),
            jax.ShapeDtypeStruct((1, inverses.shape[2]), jnp.float32),
        ),
        name="precondition",
    )(inverses, gradient)


def finish_kernel(row_ref, align_ref, momentum_ref, precond_ref, base_ref, weights_ref, next_ref):
    scale = jnp.minimum(1.0, clip_norm / jnp.sqrt(align_ref[0:1, 0:1]))
    rows = next_ref.shape[0]
    own = precond_ref[pl.ds(pl.multiple_of(row_ref[0], rows), rows), :]
    next_ref[...] = momentum_rate * momentum_ref[...] + scale * own
    weights_ref[...] = base_ref[...] - (step_rate * scale) * precond_ref[...]


def finish(first_row, align, momentum, precond, base):
    return pl.pallas_call(
        finish_kernel,
        in_specs=[pl.BlockSpec(memory_space=pltpu.SMEM)]
        + [pl.BlockSpec(memory_space=pltpu.VMEM)] * 4,
        out_shape=(
            jax.ShapeDtypeStruct(base.shape, jnp.float32),
            jax.ShapeDtypeStruct(momentum.shape, jnp.float32),
        ),
        name="finish",
    )(first_row.reshape(1).astype(jnp.int32), align, momentum, precond, base)


def after(value, first):
    return lax.optimization_barrier((value, first))[0]


def swap(value, axis, flip):
    size = lax.axis_size(axis)
    return lax.ppermute(value, axis, [(i, i ^ flip) for i in range(size)])


def exchange(value, axis):
    return [value] + [swap(value, axis, flip) for flip in range(1, lax.axis_size(axis))]


def spread(value, axis):
    copies = jnp.broadcast_to(value[None], (lax.axis_size(axis),) + value.shape)
    return lax.all_to_all(copies, axis, 0, 0)


def body(activations, grads_out, grad_parts, old_factors, block_owner, weights, momentum):
    shard_count = lax.axis_size("shards")
    replica_count = lax.axis_size("replica")
    block_count = old_factors.shape[0]
    block_size = old_factors.shape[1]
    capacity = (block_count + shard_count - 1) // shard_count + 1
    sample_count = activations.shape[0] * shard_count * lax.axis_size("tensor") * replica_count
    partial_grad = grad_parts[0]
    row_count, col_count = partial_grad.shape
    left_count = row_count // block_size
    right_count = col_count // block_size
    piece_rows = row_count // shard_count
    own_rows = weights.shape[0]
    shard = lax.axis_index("shards")
    replica = lax.axis_index("replica")

    folded = fold(sample_stats(activations, block_size), sample_stats(grads_out, block_size))
    stats_in = lax.all_to_all(folded, "shards", 0, 0)

    weights, momentum_then, old_then = after((weights, momentum, old_factors), folded)
    base_parts = exchange(weights - (step_rate * momentum_rate) * momentum_then, "replica")
    base_rows = []
    for place in range(replica_count):
        rows = base_parts[0]
        for flip in range(1, replica_count):
            rows = jnp.where(replica ^ flip == place, base_parts[flip], rows)
        base_rows.append(rows)
    base_rows = jnp.concatenate(base_rows, axis=0)
    old_block = fold_one(lax.dynamic_slice_in_dim(old_then, shard, 1, 0))
    base = lax.all_gather(base_rows, "shards", axis=0, tiled=True)

    own_stats = after(jnp.sum(stats_in, axis=0), (base_rows, old_block))
    grad_in = lax.all_to_all(
        after(partial_grad, own_stats).reshape(shard_count, piece_rows, col_count), "shards", 0, 0
    )
    own_stats = own_stats + swap(own_stats, "tensor", 1)
    own_stats = sum(exchange(own_stats, "replica"))
    own_stats = own_stats + swap(own_stats, "tensor", 2)
    blended = decay_rate * old_block + ((1.0 - decay_rate) / sample_count) * own_stats
    blended, grad_in = lax.optimization_barrier((blended, grad_in))
    folded = spread(blended, "shards")
    own_grad = sum(exchange(jnp.sum(grad_in, axis=0), "replica"))
    folded, own_grad = lax.optimization_barrier((folded, own_grad))
    gradient = spread(own_grad, "shards").reshape(row_count, col_count)

    positions = jnp.arange(block_count, dtype=jnp.int32)
    earlier = (block_owner[:, None] == block_owner[None, :]) & (
        positions[None, :] < positions[:, None]
    )
    slots = block_owner * capacity + jnp.sum(earlier.astype(jnp.int32), axis=1)
    own_slots = shard * capacity + jnp.arange(capacity, dtype=jnp.int32)
    holds = jnp.max(jnp.where(slots[None, :] == own_slots[:, None], positions[None, :], -1), axis=1)
    right_first = left_count + lax.axis_index("tensor") * right_count
    places = jnp.concatenate([right_first.reshape(1).astype(jnp.int32), holds])
    inverses, owned_blocks = invert_needed(places, folded, left_count + right_count, capacity)
    precond, align = precondition(inverses, gradient)
    align, base = lax.optimization_barrier((align, base))
    align = align + swap(align, "tensor", 1)
    align = align + swap(align, "tensor", 2)
    first_row = (shard * replica_count + replica) * own_rows
    weights_next, momentum_next = finish(first_row, align, momentum, precond, base)
    return (weights_next, momentum_next, owned_blocks)


def solution(mesh):
    placed = (
        P(("shards", "tensor", "replica"), None),
        P(("shards", "tensor", "replica"), None),
        P(("shards", "replica"), None, "tensor"),
        P(),
        P(),
        P(("shards", "replica"), "tensor"),
        P(("shards", "replica"), "tensor"),
    )
    return jax.shard_map(
        body,
        mesh=mesh,
        in_specs=placed,
        out_specs=(P(None, "tensor"), P(("shards", "replica"), "tensor"), P("shards", None, None)),
        check_vma=False,
    )
```

```python
import jax
import jax.numpy as jnp
from jax import lax
from jax.experimental import pallas as pl
from jax.experimental.pallas import tpu as pltpu
from jax.sharding import PartitionSpec as P

NS_STEPS = 4


exact_mode = lax.Precision.HIGHEST
decay_rate = 0.75
damping = 0.1
damp_shift = 0.001
clip_norm = 256.0
momentum_rate = 0.9
step_rate = 0.05


def sample_stats(samples, block_size):
    sample_rows, width = samples.shape
    blocks = samples.reshape(sample_rows, width // block_size, block_size)
    return jnp.einsum("tnb,tnc->nbc", blocks, blocks, preferred_element_type=jnp.float32)


def fold_block(block, rows):
    size = block.shape[1]
    half = size // 2
    row = lax.broadcasted_iota(jnp.int32, (half, size), 0)
    col = lax.broadcasted_iota(jnp.int32, (half, size), 1)
    top, bottom = block[:half], block[half:]
    triangle = jnp.where(col >= row, top, pltpu.roll(bottom, half, 1))
    diagonal = jnp.sum(jnp.where(col == row + half, bottom, 0.0), axis=0, keepdims=True)
    return triangle, jnp.broadcast_to(diagonal, (rows - half, size))


def fold_kernel(left_ref, right_ref, folded_ref):
    left_count, size, _ = left_ref.shape
    for n in range(folded_ref.shape[0]):
        block = left_ref[n] if n < left_count else right_ref[n - left_count]
        triangle, diagonal = fold_block(block, folded_ref.shape[1])
        folded_ref[n, : size // 2, :] = triangle
        folded_ref[n, size // 2 :, :] = diagonal


def fold(left_stats, right_stats):
    count, size, _ = left_stats.shape
    return pl.pallas_call(
        fold_kernel,
        out_shape=jax.ShapeDtypeStruct(
            (count + right_stats.shape[0], size // 2 + 8, size), jnp.float32
        ),
        name="fold",
    )(left_stats, right_stats)


def fold_one_kernel(block_ref, folded_ref):
    half = block_ref.shape[1] // 2
    triangle, diagonal = fold_block(block_ref[0], folded_ref.shape[0])
    folded_ref[:half, :] = triangle
    folded_ref[half:, :] = diagonal


def fold_one(block):
    size = block.shape[2]
    return pl.pallas_call(
        fold_one_kernel,
        out_shape=jax.ShapeDtypeStruct((size // 2 + 8, size), jnp.float32),
        name="fold_one",
    )(block)


def dot(a, b):
    return jnp.dot(a, b, precision=exact_mode, preferred_element_type=jnp.float32)


def unfold(part, diagonal):
    half, size = part.shape
    row = lax.broadcasted_iota(jnp.int32, (half, size), 0)
    col = lax.broadcasted_iota(jnp.int32, (half, size), 1)
    turned = jnp.concatenate([part, jnp.zeros_like(part)], axis=0).T
    top = jnp.where(col >= row, part, turned[:half])
    corner = jnp.where(
        col < row + half, pltpu.roll(part, half, 1), pltpu.roll(turned[:half], half, 1)
    )
    corner = jnp.where(col == row + half, diagonal, corner)
    bottom = jnp.where(col < half, turned[half:], corner)
    return jnp.concatenate([top, bottom], axis=0)


def inverse_kernel(place_ref, folded_ref, inverse_ref, owned_ref):
    needed, size, _ = inverse_ref.shape
    half = size // 2
    right_count = needed - folded_ref.shape[0] // 2
    left_count = needed - right_count

    def load(block):
        return unfold(folded_ref[block, :half, :], folded_ref[block, half : half + 1, :])

    on_diagonal = lax.broadcasted_iota(jnp.int32, (size, size), 0) == lax.broadcasted_iota(
        jnp.int32, (size, size), 1
    )
    unit = jnp.where(on_diagonal, 1.0, 0.0)
    powers, bounds, inverses = [], [], []
    for block in list(range(left_count)) + [place_ref[0] + n for n in range(right_count)]:
        mixed = load(block)
        trace = jnp.sum(jnp.where(on_diagonal, mixed, 0.0), keepdims=True)
        damped = mixed + jnp.where(on_diagonal, damping * trace / size + damp_shift, 0.0)
        bound = jnp.max(jnp.sum(jnp.abs(damped), axis=1, keepdims=True), keepdims=True)
        power = unit - damped / bound
        powers.append(power)
        bounds.append(bound)
        inverses.append(unit + power)
    for step in range(NS_STEPS - 1):
        powers = [dot(power, power) for power in powers]
        inverses = [x + dot(x, power) for x, power in zip(inverses, powers)]
    for n, (x, bound) in enumerate(zip(inverses, bounds)):
        inverse_ref[n] = x / bound

    for place in range(owned_ref.shape[0]):
        block = place_ref[1 + place]
        value = load(jnp.maximum(block, 0))
        owned_ref[place] = jnp.where(block >= 0, value, jnp.zeros_like(value))


def invert_needed(places, folded, needed, capacity):
    size = folded.shape[2]
    return pl.pallas_call(
        inverse_kernel,
        in_specs=[
            pl.BlockSpec(memory_space=pltpu.SMEM),
            pl.BlockSpec(memory_space=pltpu.VMEM),
        ],
        out_shape=(
            jax.ShapeDtypeStruct((needed, size, size), jnp.float32),
            jax.ShapeDtypeStruct((capacity, size, size), jnp.float32),
        ),
        name="inverse",
    )(places, folded)


def precondition_kernel(inverse_ref, grad_ref, precond_ref, align_ref):
    size = inverse_ref.shape[1]
    left_count = grad_ref.shape[0] // size
    right_count = grad_ref.shape[1] // size
    total = jnp.zeros((size, size), jnp.float32)
    for a in range(left_count):
        rows = slice(a * size, (a + 1) * size)
        left_part = dot(inverse_ref[a], grad_ref[rows, :])
        for c in range(right_count):
            cols = slice(c * size, (c + 1) * size)
            value = dot(left_part[:, cols], inverse_ref[left_count + c])
            precond_ref[rows, cols] = value
            total = total + value * grad_ref[rows, cols]
    align_ref[...] = jnp.broadcast_to(jnp.sum(total, keepdims=True), align_ref.shape)


def precondition(inverses, gradient):
    return pl.pallas_call(
        precondition_kernel,
        out_shape=(
            jax.ShapeDtypeStruct(gradient.shape, jnp.float32),
            jax.ShapeDtypeStruct((1, inverses.shape[2]), jnp.float32),
        ),
        name="precondition",
    )(inverses, gradient)


def finish_kernel(row_ref, align_ref, momentum_ref, precond_ref, base_ref, weights_ref, next_ref):
    scale = jnp.minimum(1.0, clip_norm / jnp.sqrt(align_ref[0:1, 0:1]))
    rows = next_ref.shape[0]
    own = precond_ref[pl.ds(pl.multiple_of(row_ref[0], rows), rows), :]
    next_ref[...] = momentum_rate * momentum_ref[...] + scale * own
    weights_ref[...] = base_ref[...] - (step_rate * scale) * precond_ref[...]


def finish(first_row, align, momentum, precond, base):
    return pl.pallas_call(
        finish_kernel,
        in_specs=[pl.BlockSpec(memory_space=pltpu.SMEM)]
        + [pl.BlockSpec(memory_space=pltpu.VMEM)] * 4,
        out_shape=(
            jax.ShapeDtypeStruct(base.shape, jnp.float32),
            jax.ShapeDtypeStruct(momentum.shape, jnp.float32),
        ),
        name="finish",
    )(first_row.reshape(1).astype(jnp.int32), align, momentum, precond, base)


def after(value, first):
    return lax.optimization_barrier((value, first))[0]


def swap(value, axis, flip):
    size = lax.axis_size(axis)
    return lax.ppermute(value, axis, [(i, i ^ flip) for i in range(size)])


def exchange(value, axis):
    return [value] + [swap(value, axis, flip) for flip in range(1, lax.axis_size(axis))]


def spread(value, axis):
    copies = jnp.broadcast_to(value[None], (lax.axis_size(axis),) + value.shape)
    return lax.all_to_all(copies, axis, 0, 0)


def body(activations, grads_out, grad_parts, old_factors, block_owner, weights, momentum):
    shard_count = lax.axis_size("shards")
    replica_count = lax.axis_size("replica")
    block_count = old_factors.shape[0]
    block_size = old_factors.shape[1]
    capacity = (block_count + shard_count - 1) // shard_count + 1
    sample_count = activations.shape[0] * shard_count * lax.axis_size("tensor") * replica_count
    partial_grad = grad_parts[0]
    row_count, col_count = partial_grad.shape
    left_count = row_count // block_size
    right_count = col_count // block_size
    piece_rows = row_count // shard_count
    own_rows = weights.shape[0]
    shard = lax.axis_index("shards")
    replica = lax.axis_index("replica")

    folded = fold(sample_stats(activations, block_size), sample_stats(grads_out, block_size))
    stats_in = lax.all_to_all(folded, "shards", 0, 0)

    weights, momentum_then, old_then = after((weights, momentum, old_factors), folded)
    base_parts = exchange(weights - (step_rate * momentum_rate) * momentum_then, "replica")
    base_rows = []
    for place in range(replica_count):
        rows = base_parts[0]
        for flip in range(1, replica_count):
            rows = jnp.where(replica ^ flip == place, base_parts[flip], rows)
        base_rows.append(rows)
    base_rows = jnp.concatenate(base_rows, axis=0)
    old_block = fold_one(lax.dynamic_slice_in_dim(old_then, shard, 1, 0))

    own_stats = after(jnp.sum(stats_in, axis=0), (base_rows, old_block))
    grad_in = lax.all_to_all(
        after(partial_grad, own_stats).reshape(shard_count, piece_rows, col_count), "shards", 0, 0
    )
    own_stats = own_stats + swap(own_stats, "tensor", 1)
    own_stats = sum(exchange(own_stats, "replica"))
    own_stats = own_stats + swap(own_stats, "tensor", 2)
    blended = decay_rate * old_block + ((1.0 - decay_rate) / sample_count) * own_stats
    blended, grad_in = lax.optimization_barrier((blended, grad_in))
    folded = spread(blended, "shards")
    own_grad = sum(exchange(jnp.sum(grad_in, axis=0), "replica"))
    folded, own_grad = lax.optimization_barrier((folded, own_grad))
    gradient = spread(own_grad, "shards").reshape(row_count, col_count)

    positions = jnp.arange(block_count, dtype=jnp.int32)
    earlier = (block_owner[:, None] == block_owner[None, :]) & (
        positions[None, :] < positions[:, None]
    )
    slots = block_owner * capacity + jnp.sum(earlier.astype(jnp.int32), axis=1)
    own_slots = shard * capacity + jnp.arange(capacity, dtype=jnp.int32)
    holds = jnp.max(jnp.where(slots[None, :] == own_slots[:, None], positions[None, :], -1), axis=1)
    right_first = left_count + lax.axis_index("tensor") * right_count
    places = jnp.concatenate([right_first.reshape(1).astype(jnp.int32), holds])
    inverses, owned_blocks = invert_needed(places, folded, left_count + right_count, capacity)
    base_copies = jnp.broadcast_to(
        after(base_rows, inverses)[None], (shard_count,) + base_rows.shape
    )
    inverses, gradient = lax.optimization_barrier((inverses, gradient))
    base = lax.all_to_all(after(base_copies, gradient), "shards", 0, 0).reshape(
        row_count, col_count
    )
    precond, align = precondition(inverses, gradient)
    align = align + swap(align, "tensor", 1)
    align = align + swap(align, "tensor", 2)
    first_row = (shard * replica_count + replica) * own_rows
    weights_next, momentum_next = finish(first_row, align, momentum, precond, base)
    return (weights_next, momentum_next, owned_blocks)


def solution(mesh):
    placed = (
        P(("shards", "tensor", "replica"), None),
        P(("shards", "tensor", "replica"), None),
        P(("shards", "replica"), None, "tensor"),
        P(),
        P(),
        P(("shards", "replica"), "tensor"),
        P(("shards", "replica"), "tensor"),
    )
    return jax.shard_map(
        body,
        mesh=mesh,
        in_specs=placed,
        out_specs=(P(None, "tensor"), P(("shards", "replica"), "tensor"), P("shards", None, None)),
        check_vma=False,
    )
```

```python
import jax
import jax.numpy as jnp
from jax import lax
from jax.experimental import pallas as pl
from jax.experimental.pallas import tpu as pltpu
from jax.sharding import PartitionSpec as P

NS_STEPS = 4


exact_mode = lax.Precision.HIGHEST
decay_rate = 0.75
damping = 0.1
damp_shift = 0.001
clip_norm = 256.0
momentum_rate = 0.9
step_rate = 0.05


def sample_stats(samples, block_size):
    sample_rows, width = samples.shape
    blocks = samples.reshape(sample_rows, width // block_size, block_size)
    return jnp.einsum("tnb,tnc->nbc", blocks, blocks, preferred_element_type=jnp.float32)


def fold_block(block, rows):
    size = block.shape[1]
    half = size // 2
    row = lax.broadcasted_iota(jnp.int32, (half, size), 0)
    col = lax.broadcasted_iota(jnp.int32, (half, size), 1)
    top, bottom = block[:half], block[half:]
    triangle = jnp.where(col >= row, top, pltpu.roll(bottom, half, 1))
    diagonal = jnp.sum(jnp.where(col == row + half, bottom, 0.0), axis=0, keepdims=True)
    return triangle, jnp.broadcast_to(diagonal, (rows - half, size))


def fold_kernel(left_ref, right_ref, folded_ref):
    left_count, size, _ = left_ref.shape
    for n in range(folded_ref.shape[0]):
        block = left_ref[n] if n < left_count else right_ref[n - left_count]
        triangle, diagonal = fold_block(block, folded_ref.shape[1])
        folded_ref[n, : size // 2, :] = triangle
        folded_ref[n, size // 2 :, :] = diagonal


def fold(left_stats, right_stats):
    count, size, _ = left_stats.shape
    return pl.pallas_call(
        fold_kernel,
        out_shape=jax.ShapeDtypeStruct(
            (count + right_stats.shape[0], size // 2 + 8, size), jnp.float32
        ),
        name="fold",
    )(left_stats, right_stats)


def fold_one_kernel(block_ref, folded_ref):
    half = block_ref.shape[1] // 2
    triangle, diagonal = fold_block(block_ref[0], folded_ref.shape[0])
    folded_ref[:half, :] = triangle
    folded_ref[half:, :] = diagonal


def fold_one(block):
    size = block.shape[2]
    return pl.pallas_call(
        fold_one_kernel,
        out_shape=jax.ShapeDtypeStruct((size // 2 + 8, size), jnp.float32),
        name="fold_one",
    )(block)


def dot(a, b):
    return jnp.dot(a, b, precision=exact_mode, preferred_element_type=jnp.float32)


def unfold(part, diagonal):
    half, size = part.shape
    row = lax.broadcasted_iota(jnp.int32, (half, size), 0)
    col = lax.broadcasted_iota(jnp.int32, (half, size), 1)
    turned = jnp.concatenate([part, jnp.zeros_like(part)], axis=0).T
    top = jnp.where(col >= row, part, turned[:half])
    corner = jnp.where(
        col < row + half, pltpu.roll(part, half, 1), pltpu.roll(turned[:half], half, 1)
    )
    corner = jnp.where(col == row + half, diagonal, corner)
    bottom = jnp.where(col < half, turned[half:], corner)
    return jnp.concatenate([top, bottom], axis=0)


def inverse_kernel(place_ref, folded_ref, inverse_ref, owned_ref):
    needed, size, _ = inverse_ref.shape
    half = size // 2
    right_count = needed - folded_ref.shape[0] // 2
    left_count = needed - right_count

    def load(block):
        return unfold(folded_ref[block, :half, :], folded_ref[block, half : half + 1, :])

    on_diagonal = lax.broadcasted_iota(jnp.int32, (size, size), 0) == lax.broadcasted_iota(
        jnp.int32, (size, size), 1
    )
    unit = jnp.where(on_diagonal, 1.0, 0.0)
    powers, bounds, inverses = [], [], []
    for block in list(range(left_count)) + [place_ref[0] + n for n in range(right_count)]:
        mixed = load(block)
        trace = jnp.sum(jnp.where(on_diagonal, mixed, 0.0), keepdims=True)
        damped = mixed + jnp.where(on_diagonal, damping * trace / size + damp_shift, 0.0)
        bound = jnp.max(jnp.sum(jnp.abs(damped), axis=1, keepdims=True), keepdims=True)
        power = unit - damped / bound
        powers.append(power)
        bounds.append(bound)
        inverses.append(unit + power)
    for step in range(NS_STEPS - 1):
        powers = [dot(power, power) for power in powers]
        inverses = [x + dot(x, power) for x, power in zip(inverses, powers)]
    for n, (x, bound) in enumerate(zip(inverses, bounds)):
        inverse_ref[n] = x / bound

    for place in range(owned_ref.shape[0]):
        block = place_ref[1 + place]
        value = load(jnp.maximum(block, 0))
        owned_ref[place] = jnp.where(block >= 0, value, jnp.zeros_like(value))


def invert_needed(places, folded, needed, capacity):
    size = folded.shape[2]
    return pl.pallas_call(
        inverse_kernel,
        in_specs=[
            pl.BlockSpec(memory_space=pltpu.SMEM),
            pl.BlockSpec(memory_space=pltpu.VMEM),
        ],
        out_shape=(
            jax.ShapeDtypeStruct((needed, size, size), jnp.float32),
            jax.ShapeDtypeStruct((capacity, size, size), jnp.float32),
        ),
        name="inverse",
    )(places, folded)


def precondition_kernel(inverse_ref, grad_ref, precond_ref, align_ref):
    size = inverse_ref.shape[1]
    left_count = grad_ref.shape[0] // size
    right_count = grad_ref.shape[1] // size
    total = jnp.zeros((size, size), jnp.float32)
    for a in range(left_count):
        rows = slice(a * size, (a + 1) * size)
        left_part = dot(inverse_ref[a], grad_ref[rows, :])
        for c in range(right_count):
            cols = slice(c * size, (c + 1) * size)
            value = dot(left_part[:, cols], inverse_ref[left_count + c])
            precond_ref[rows, cols] = value
            total = total + value * grad_ref[rows, cols]
    align_ref[...] = jnp.broadcast_to(jnp.sum(total, keepdims=True), align_ref.shape)


def precondition(inverses, gradient):
    return pl.pallas_call(
        precondition_kernel,
        out_shape=(
            jax.ShapeDtypeStruct(gradient.shape, jnp.float32),
            jax.ShapeDtypeStruct((1, inverses.shape[2]), jnp.float32),
        ),
        name="precondition",
    )(inverses, gradient)


def finish_kernel(
    row_ref, align_ref, other_ref, momentum_ref, precond_ref, base_ref, weights_ref, next_ref
):
    total = align_ref[0:1, 0:1] + other_ref[0:1, 0:1]
    scale = jnp.minimum(1.0, clip_norm / jnp.sqrt(total))
    own_rows = next_ref.shape[0]
    first = row_ref[0] - pl.program_id(0) * precond_ref.shape[0]
    weights_ref[...] = base_ref[...] - (step_rate * scale) * precond_ref[...]

    @pl.when((first >= 0) & (first < precond_ref.shape[0]))
    def _():
        own = precond_ref[pl.ds(pl.multiple_of(first, own_rows), own_rows), :]
        next_ref[...] = momentum_rate * momentum_ref[...] + scale * own


def finish(first_row, align, other, momentum, precond, base, steps=4):
    rows, cols = base.shape
    whole = lambda value: pl.BlockSpec(value.shape, lambda i: (0, 0))
    part = pl.BlockSpec((rows // steps, cols), lambda i: (i, 0))
    return pl.pallas_call(
        finish_kernel,
        grid=(steps,),
        in_specs=[
            pl.BlockSpec(memory_space=pltpu.SMEM),
            whole(align),
            whole(other),
            whole(momentum),
            part,
            part,
        ],
        out_specs=(part, whole(momentum)),
        out_shape=(
            jax.ShapeDtypeStruct(base.shape, jnp.float32),
            jax.ShapeDtypeStruct(momentum.shape, jnp.float32),
        ),
        name="finish",
    )(first_row.reshape(1).astype(jnp.int32), align, other, momentum, precond, base)


def after(value, first):
    return lax.optimization_barrier((value, first))[0]


def swap(value, axis, flip):
    size = lax.axis_size(axis)
    return lax.ppermute(value, axis, [(i, i ^ flip) for i in range(size)])


def exchange(value, axis):
    return [value] + [swap(value, axis, flip) for flip in range(1, lax.axis_size(axis))]


def spread(value, axis):
    copies = jnp.broadcast_to(value[None], (lax.axis_size(axis),) + value.shape)
    return lax.all_to_all(copies, axis, 0, 0)


def body(activations, grads_out, grad_parts, old_factors, block_owner, weights, momentum):
    shard_count = lax.axis_size("shards")
    replica_count = lax.axis_size("replica")
    block_count = old_factors.shape[0]
    block_size = old_factors.shape[1]
    capacity = (block_count + shard_count - 1) // shard_count + 1
    sample_count = activations.shape[0] * shard_count * lax.axis_size("tensor") * replica_count
    partial_grad = grad_parts[0]
    row_count, col_count = partial_grad.shape
    left_count = row_count // block_size
    right_count = col_count // block_size
    piece_rows = row_count // shard_count
    own_rows = weights.shape[0]
    shard = lax.axis_index("shards")
    replica = lax.axis_index("replica")

    folded = fold(sample_stats(activations, block_size), sample_stats(grads_out, block_size))
    stats_in = lax.all_to_all(folded, "shards", 0, 0)

    weights, momentum_then, old_then = after((weights, momentum, old_factors), folded)
    base_parts = exchange(weights - (step_rate * momentum_rate) * momentum_then, "replica")
    base_rows = []
    for place in range(replica_count):
        rows = base_parts[0]
        for flip in range(1, replica_count):
            rows = jnp.where(replica ^ flip == place, base_parts[flip], rows)
        base_rows.append(rows)
    base_rows = jnp.concatenate(base_rows, axis=0)
    old_block = fold_one(lax.dynamic_slice_in_dim(old_then, shard, 1, 0))

    own_stats = after(jnp.sum(stats_in, axis=0), (base_rows, old_block))
    grad_in = lax.all_to_all(
        after(partial_grad, own_stats).reshape(shard_count, piece_rows, col_count), "shards", 0, 0
    )
    own_stats = own_stats + swap(own_stats, "tensor", 1)
    own_stats = sum(exchange(own_stats, "replica"))
    own_stats = own_stats + swap(own_stats, "tensor", 2)
    blended = decay_rate * old_block + ((1.0 - decay_rate) / sample_count) * own_stats
    blended, grad_in = lax.optimization_barrier((blended, grad_in))
    folded = spread(blended, "shards")
    own_grad = sum(exchange(jnp.sum(grad_in, axis=0), "replica"))
    folded, own_grad = lax.optimization_barrier((folded, own_grad))
    gradient = spread(own_grad, "shards").reshape(row_count, col_count)

    positions = jnp.arange(block_count, dtype=jnp.int32)
    earlier = (block_owner[:, None] == block_owner[None, :]) & (
        positions[None, :] < positions[:, None]
    )
    slots = block_owner * capacity + jnp.sum(earlier.astype(jnp.int32), axis=1)
    own_slots = shard * capacity + jnp.arange(capacity, dtype=jnp.int32)
    holds = jnp.max(jnp.where(slots[None, :] == own_slots[:, None], positions[None, :], -1), axis=1)
    right_first = left_count + lax.axis_index("tensor") * right_count
    places = jnp.concatenate([right_first.reshape(1).astype(jnp.int32), holds])
    places = after(places, folded)
    base_copies = jnp.broadcast_to(
        after(base_rows, places)[None], (shard_count,) + base_rows.shape
    )
    places = after(places, base_copies)
    inverses, owned_blocks = invert_needed(places, folded, left_count + right_count, capacity)
    inverses, gradient = lax.optimization_barrier((inverses, gradient))
    base = lax.all_to_all(after(base_copies, gradient), "shards", 0, 0).reshape(
        row_count, col_count
    )
    precond, align = precondition(inverses, gradient)
    align = align + swap(align, "tensor", 1)
    first_row = (shard * replica_count + replica) * own_rows
    weights_next, momentum_next = finish(
        first_row, align, swap(align, "tensor", 2), momentum, precond, base
    )
    return (weights_next, momentum_next, owned_blocks)


def solution(mesh):
    placed = (
        P(("shards", "tensor", "replica"), None),
        P(("shards", "tensor", "replica"), None),
        P(("shards", "replica"), None, "tensor"),
        P(),
        P(),
        P(("shards", "replica"), "tensor"),
        P(("shards", "replica"), "tensor"),
    )
    return jax.shard_map(
        body,
        mesh=mesh,
        in_specs=placed,
        out_specs=(P(None, "tensor"), P(("shards", "replica"), "tensor"), P("shards", None, None)),
        check_vma=False,
    )
```

```python
import jax
import jax.numpy as jnp
from jax import lax
from jax.experimental import pallas as pl
from jax.experimental.pallas import tpu as pltpu
from jax.sharding import PartitionSpec as P

NS_STEPS = 4


exact_mode = lax.Precision.HIGHEST
decay_rate = 0.75
damping = 0.1
damp_shift = 0.001
clip_norm = 256.0
momentum_rate = 0.9
step_rate = 0.05


def sample_stats(samples, block_size):
    sample_rows, width = samples.shape
    blocks = samples.reshape(sample_rows, width // block_size, block_size)
    return jnp.einsum("tnb,tnc->nbc", blocks, blocks, preferred_element_type=jnp.float32)


def fold_block(block, rows):
    size = block.shape[1]
    half = size // 2
    row = lax.broadcasted_iota(jnp.int32, (half, size), 0)
    col = lax.broadcasted_iota(jnp.int32, (half, size), 1)
    top, bottom = block[:half], block[half:]
    triangle = jnp.where(col >= row, top, pltpu.roll(bottom, half, 1))
    diagonal = jnp.sum(jnp.where(col == row + half, bottom, 0.0), axis=0, keepdims=True)
    return triangle, jnp.broadcast_to(diagonal, (rows - half, size))


def fold_kernel(left_ref, right_ref, folded_ref):
    left_count, size, _ = left_ref.shape
    for n in range(folded_ref.shape[0]):
        block = left_ref[n] if n < left_count else right_ref[n - left_count]
        triangle, diagonal = fold_block(block, folded_ref.shape[1])
        folded_ref[n, : size // 2, :] = triangle
        folded_ref[n, size // 2 :, :] = diagonal


def fold(left_stats, right_stats):
    count, size, _ = left_stats.shape
    return pl.pallas_call(
        fold_kernel,
        out_shape=jax.ShapeDtypeStruct(
            (count + right_stats.shape[0], size // 2 + 8, size), jnp.float32
        ),
        name="fold",
    )(left_stats, right_stats)


def fold_one_kernel(block_ref, folded_ref):
    half = block_ref.shape[1] // 2
    triangle, diagonal = fold_block(block_ref[0], folded_ref.shape[0])
    folded_ref[:half, :] = triangle
    folded_ref[half:, :] = diagonal


def fold_one(block):
    size = block.shape[2]
    return pl.pallas_call(
        fold_one_kernel,
        out_shape=jax.ShapeDtypeStruct((size // 2 + 8, size), jnp.float32),
        name="fold_one",
    )(block)


def dot(a, b):
    return jnp.dot(a, b, precision=exact_mode, preferred_element_type=jnp.float32)


def unfold(part, diagonal):
    half, size = part.shape
    row = lax.broadcasted_iota(jnp.int32, (half, size), 0)
    col = lax.broadcasted_iota(jnp.int32, (half, size), 1)
    turned = jnp.concatenate([part, jnp.zeros_like(part)], axis=0).T
    top = jnp.where(col >= row, part, turned[:half])
    corner = jnp.where(
        col < row + half, pltpu.roll(part, half, 1), pltpu.roll(turned[:half], half, 1)
    )
    corner = jnp.where(col == row + half, diagonal, corner)
    bottom = jnp.where(col < half, turned[half:], corner)
    return jnp.concatenate([top, bottom], axis=0)


def inverse_kernel(place_ref, folded_ref, inverse_ref, owned_ref):
    needed, size, _ = inverse_ref.shape
    half = size // 2
    right_count = needed - folded_ref.shape[0] // 2
    left_count = needed - right_count

    def load(block):
        return unfold(folded_ref[block, :half, :], folded_ref[block, half : half + 1, :])

    on_diagonal = lax.broadcasted_iota(jnp.int32, (size, size), 0) == lax.broadcasted_iota(
        jnp.int32, (size, size), 1
    )
    unit = jnp.where(on_diagonal, 1.0, 0.0)
    powers, bounds, inverses = [], [], []
    for block in list(range(left_count)) + [place_ref[0] + n for n in range(right_count)]:
        mixed = load(block)
        trace = jnp.sum(jnp.where(on_diagonal, mixed, 0.0), keepdims=True)
        damped = mixed + jnp.where(on_diagonal, damping * trace / size + damp_shift, 0.0)
        bound = jnp.max(jnp.sum(jnp.abs(damped), axis=1, keepdims=True), keepdims=True)
        power = unit - damped / bound
        powers.append(power)
        bounds.append(bound)
        inverses.append(unit + power)
    for step in range(NS_STEPS - 1):
        powers = [dot(power, power) for power in powers]
        inverses = [x + dot(x, power) for x, power in zip(inverses, powers)]
    for n, (x, bound) in enumerate(zip(inverses, bounds)):
        inverse_ref[n] = x / bound

    for place in range(owned_ref.shape[0]):
        block = place_ref[1 + place]
        value = load(jnp.maximum(block, 0))
        owned_ref[place] = jnp.where(block >= 0, value, jnp.zeros_like(value))


def invert_needed(places, folded, needed, capacity):
    size = folded.shape[2]
    return pl.pallas_call(
        inverse_kernel,
        in_specs=[
            pl.BlockSpec(memory_space=pltpu.SMEM),
            pl.BlockSpec(memory_space=pltpu.VMEM),
        ],
        out_shape=(
            jax.ShapeDtypeStruct((needed, size, size), jnp.float32),
            jax.ShapeDtypeStruct((capacity, size, size), jnp.float32),
        ),
        name="inverse",
    )(places, folded)


def precondition_kernel(inverse_ref, grad_ref, precond_ref, align_ref):
    size = inverse_ref.shape[1]
    left_count = grad_ref.shape[0] // size
    right_count = grad_ref.shape[1] // size
    total = jnp.zeros((size, size), jnp.float32)
    for a in range(left_count):
        rows = slice(a * size, (a + 1) * size)
        left_part = dot(inverse_ref[a], grad_ref[rows, :])
        for c in range(right_count):
            cols = slice(c * size, (c + 1) * size)
            value = dot(left_part[:, cols], inverse_ref[left_count + c])
            precond_ref[rows, cols] = value
            total = total + value * grad_ref[rows, cols]
    align_ref[...] = jnp.broadcast_to(jnp.sum(total, keepdims=True), align_ref.shape)


def precondition(inverses, gradient):
    return pl.pallas_call(
        precondition_kernel,
        out_shape=(
            jax.ShapeDtypeStruct(gradient.shape, jnp.float32),
            jax.ShapeDtypeStruct((1, inverses.shape[2]), jnp.float32),
        ),
        name="precondition",
    )(inverses, gradient)


def finish_kernel(
    row_ref, align_ref, other_ref, momentum_ref, precond_ref, base_ref, weights_ref, next_ref
):
    total = align_ref[0:1, 0:1] + other_ref[0:1, 0:1]
    scale = jnp.minimum(1.0, clip_norm / jnp.sqrt(total))
    rows = next_ref.shape[0]
    own = precond_ref[pl.ds(pl.multiple_of(row_ref[0], rows), rows), :]
    next_ref[...] = momentum_rate * momentum_ref[...] + scale * own
    weights_ref[...] = base_ref[...] - (step_rate * scale) * precond_ref[...]


def finish(first_row, align, other, momentum, precond, base):
    return pl.pallas_call(
        finish_kernel,
        in_specs=[pl.BlockSpec(memory_space=pltpu.SMEM)]
        + [pl.BlockSpec(memory_space=pltpu.VMEM)] * 5,
        out_shape=(
            jax.ShapeDtypeStruct(base.shape, jnp.float32),
            jax.ShapeDtypeStruct(momentum.shape, jnp.float32),
        ),
        name="finish",
    )(first_row.reshape(1).astype(jnp.int32), align, other, momentum, precond, base)


def after(value, first):
    return lax.optimization_barrier((value, first))[0]


def swap(value, axis, flip):
    size = lax.axis_size(axis)
    return lax.ppermute(value, axis, [(i, i ^ flip) for i in range(size)])


def exchange(value, axis):
    return [value] + [swap(value, axis, flip) for flip in range(1, lax.axis_size(axis))]


def spread(value, axis):
    copies = jnp.broadcast_to(value[None], (lax.axis_size(axis),) + value.shape)
    return lax.all_to_all(copies, axis, 0, 0)


def body(activations, grads_out, grad_parts, old_factors, block_owner, weights, momentum):
    shard_count = lax.axis_size("shards")
    replica_count = lax.axis_size("replica")
    block_count = old_factors.shape[0]
    block_size = old_factors.shape[1]
    capacity = (block_count + shard_count - 1) // shard_count + 1
    sample_count = activations.shape[0] * shard_count * lax.axis_size("tensor") * replica_count
    partial_grad = grad_parts[0]
    row_count, col_count = partial_grad.shape
    left_count = row_count // block_size
    right_count = col_count // block_size
    piece_rows = row_count // shard_count
    own_rows = weights.shape[0]
    shard = lax.axis_index("shards")
    replica = lax.axis_index("replica")

    folded = fold(sample_stats(activations, block_size), sample_stats(grads_out, block_size))
    stats_in = lax.all_to_all(folded, "shards", 0, 0)

    weights, momentum_then, old_then = after((weights, momentum, old_factors), folded)
    base_parts = exchange(weights - (step_rate * momentum_rate) * momentum_then, "replica")
    base_rows = []
    for place in range(replica_count):
        rows = base_parts[0]
        for flip in range(1, replica_count):
            rows = jnp.where(replica ^ flip == place, base_parts[flip], rows)
        base_rows.append(rows)
    base_rows = jnp.concatenate(base_rows, axis=0)
    old_block = fold_one(lax.dynamic_slice_in_dim(old_then, shard, 1, 0))

    own_stats = after(jnp.sum(stats_in, axis=0), (base_rows, old_block))
    grad_in = lax.all_to_all(
        after(partial_grad, own_stats).reshape(shard_count, piece_rows, col_count), "shards", 0, 0
    )
    own_stats = own_stats + swap(own_stats, "tensor", 1)
    own_stats = sum(exchange(own_stats, "replica"))
    own_stats = own_stats + swap(own_stats, "tensor", 2)
    blended = decay_rate * old_block + ((1.0 - decay_rate) / sample_count) * own_stats
    blended, grad_in = lax.optimization_barrier((blended, grad_in))
    folded = spread(blended, "shards")
    own_grad = sum(exchange(jnp.sum(grad_in, axis=0), "replica"))
    folded, own_grad = lax.optimization_barrier((folded, own_grad))
    gradient = spread(own_grad, "shards").reshape(row_count, col_count)

    positions = jnp.arange(block_count, dtype=jnp.int32)
    earlier = (block_owner[:, None] == block_owner[None, :]) & (
        positions[None, :] < positions[:, None]
    )
    slots = block_owner * capacity + jnp.sum(earlier.astype(jnp.int32), axis=1)
    own_slots = shard * capacity + jnp.arange(capacity, dtype=jnp.int32)
    holds = jnp.max(jnp.where(slots[None, :] == own_slots[:, None], positions[None, :], -1), axis=1)
    right_first = left_count + lax.axis_index("tensor") * right_count
    places = jnp.concatenate([right_first.reshape(1).astype(jnp.int32), holds])
    places = after(places, folded)
    base_copies = jnp.broadcast_to(
        after(base_rows, places)[None], (shard_count,) + base_rows.shape
    )
    places = after(places, base_copies)
    inverses, owned_blocks = invert_needed(places, folded, left_count + right_count, capacity)
    inverses, gradient = lax.optimization_barrier((inverses, gradient))
    base = lax.all_to_all(after(base_copies, gradient), "shards", 0, 0).reshape(
        row_count, col_count
    )
    precond, align = precondition(inverses, gradient)
    align = align + swap(align, "tensor", 1)
    first_row = (shard * replica_count + replica) * own_rows
    weights_next, momentum_next = finish(
        first_row, align, swap(align, "tensor", 2), momentum, precond, base
    )
    return (weights_next, momentum_next, owned_blocks)


def solution(mesh):
    placed = (
        P(("shards", "tensor", "replica"), None),
        P(("shards", "tensor", "replica"), None),
        P(("shards", "replica"), None, "tensor"),
        P(),
        P(),
        P(("shards", "replica"), "tensor"),
        P(("shards", "replica"), "tensor"),
    )
    return jax.shard_map(
        body,
        mesh=mesh,
        in_specs=placed,
        out_specs=(P(None, "tensor"), P(("shards", "replica"), "tensor"), P("shards", None, None)),
        check_vma=False,
    )
```
